256 devices in a mesh: dp: 16 (over z_lo, x), seq: 16 (over y, z_hi, core).
Axes of the slice: x: 4, y: 4, z: 8 (z_hi: 2, z_lo: 4; z = z_hi * 4 + z_lo), core: 2. Of those that a mesh axis runs over, the one named last changes fastest.
Arguments:
- hidden: bfloat16 [16, 2048, 5120], P('dp', 'seq'), may hold values from -6 to 6
- queries: bfloat16 [16, 2048, 2560], P('dp', 'seq'), may hold values from -9 to 9
- keys: bfloat16 [16, 2048, 512], P('dp', 'seq'), may hold values from -9 to 9
- value_weight: bfloat16 [5120, 512], P('dp'), may hold values from -0.078125 to 0.078125
- doc_ids: int32 [16, 2048], P('dp', 'seq'), may hold values from 0 to 3, never falling along the last dimension, each value on 1 to 1024 neighbouring positions
- cotangent: bfloat16 [16, 2048, 2560], P('dp', 'seq'), may hold values from -6 to 6
Outputs:
- attn_out: bfloat16 [16, 2048, 2560], P('dp', 'seq')
- grad_queries: bfloat16 [16, 2048, 2560], P('dp', 'seq')
- grad_keys: bfloat16 [16, 2048, 512], P('dp', 'seq')
- grad_hidden: bfloat16 [16, 2048, 5120], P('dp', 'seq')
- grad_weight: float32 [5120, 512], P('dp')
The draws below stay inside these ranges and needn't reach their ends.
Inputs may be any that keep to these rules, and one draw needn't show every extreme that they name: `doc_ids`: document numbers never fall along a span; one document has exactly 1024 tokens, none more.
All inputs are finite; a program needn't handle non-finite values.
Results may differ from the reference program's by a relative error of at most 0.025.
Values may be sent and summed in bfloat16 or wider, within the bound.
A program may use at most 128 MiB of HBM per device.

```python
import math
import jax
import jax.numpy as jnp
import numpy as np
from jax import lax

D = 5120
QUERY_HEADS = 20
KEY_VALUE_HEADS = 4
HEAD_SIZE = 128
TOKENS_PER_SLOT = 128
QUERY_PER_KV = 5
KW = 512
QW = 2560
SPAN_TOKENS = 2048
SPAN_COUNT = 16
N_SEQ = 16


def shift_back(source, shifted_by):
    padding = jnp.zeros_like(source[:, :shifted_by])
    return jnp.concatenate((source[:, shifted_by:], padding), axis=1)


def planted_pair(key):
    base_key = jax.random.fold_in(key, 5171)
    flow_list = jax.random.split(base_key, 7)
    query_layout = (SPAN_COUNT, SPAN_TOKENS, KEY_VALUE_HEADS, QUERY_PER_KV, HEAD_SIZE)
    key_layout = (SPAN_COUNT, SPAN_TOKENS, KEY_VALUE_HEADS, HEAD_SIZE)
    query_base = 1.5 * jnp.clip(jax.random.normal(flow_list[0], query_layout, jnp.float32), -6.0, 6.0)
    key_base = 1.5 * jnp.clip(jax.random.normal(flow_list[1], key_layout, jnp.float32), -6.0, 6.0)
    stride = max(SPAN_TOKENS // 4, 2)
    block_list = SPAN_TOKENS // stride
    offsets = jax.random.randint(flow_list[2], (SPAN_COUNT, block_list), 1, stride)
    picked_rows = jax.random.randint(flow_list[3], (SPAN_COUNT, block_list), 0, KEY_VALUE_HEADS)
    position = jnp.arange(SPAN_TOKENS, dtype=jnp.int32)
    block_lookup = jnp.minimum(position // stride, block_list - 1)
    flagged_rows = (position[None, :] % stride == offsets[:, block_lookup]) & (position[None, :] // stride < block_list) & (position[None, :] > TOKENS_PER_SLOT)
    head_marker = flagged_rows[:, :, None] & (picked_rows[:, block_lookup][:, :, None] == jnp.arange(KEY_VALUE_HEADS, dtype=jnp.int32)[None, None, :])
    sign_table = jax.random.rademacher(flow_list[4], key_layout, jnp.float32)
    signal_strength = jax.random.uniform(flow_list[5], (SPAN_COUNT, SPAN_TOKENS, KEY_VALUE_HEADS, QUERY_PER_KV, 1), jnp.float32, 0.4, 1.0)
    score_margin = jax.random.uniform(flow_list[6], (SPAN_COUNT, SPAN_TOKENS, KEY_VALUE_HEADS, 1), jnp.float32, 2.5, 3.0)
    magnitude = math.sqrt(300.0) * HEAD_SIZE ** (-0.25)
    queries = jnp.where(head_marker[..., None, None], signal_strength * magnitude * sign_table[:, :, :, None, :], query_base)
    main_mark = shift_back(head_marker, TOKENS_PER_SLOT)
    second_mark = shift_back(head_marker, TOKENS_PER_SLOT + 1)
    main_keys = magnitude * shift_back(sign_table, TOKENS_PER_SLOT)
    second_keys = magnitude * (1.0 - shift_back(score_margin, TOKENS_PER_SLOT + 1) / 300.0) * shift_back(sign_table, TOKENS_PER_SLOT + 1)
    keys = jnp.where(main_mark[..., None], main_keys, jnp.where(second_mark[..., None], second_keys, key_base))
    return (queries.reshape(SPAN_COUNT, SPAN_TOKENS, QUERY_HEADS * HEAD_SIZE), keys.reshape(SPAN_COUNT, SPAN_TOKENS, KEY_VALUE_HEADS * HEAD_SIZE))


def draw_queries(key, part):
    return planted_pair(key)[0].astype(jnp.bfloat16)


def draw_keys(key, part):
    return planted_pair(key)[1].astype(jnp.bfloat16)


def with_spikes(values, rng, source, target, blocks, factor):
    owner, partner = [(jnp.arange(values.shape[axis_at]) // (values.shape[axis_at] // blocks)).reshape([-1 if axis == axis_at else 1 for axis in range(values.ndim)]) for axis_at in (source, target)]
    chosen = jax.random.permutation(rng, blocks)[partner]
    strong = (owner == chosen) | (owner == (partner + blocks // 2) % blocks)
    return jnp.where(strong, factor * values, values)


def steps_of(stream_key, shape, cuts, smallest, top_value):
    def one(dim, shards_of):
        steps = jax.random.uniform(jax.random.fold_in(jax.random.fold_in(stream_key, 6), dim), (shards_of,), jnp.float32, smallest / len(cuts), top_value / len(cuts))
        return jnp.repeat(jnp.exp(steps), shape[dim] // shards_of).reshape((-1,) + (1,) * (len(shape) - dim - 1))

    gain = one(*cuts[0])
    for cut in cuts[1:]:
        gain = gain * one(*cut)
    return gain


def length_profile(count, total, limit, lean):
    weights = [(1 << 20) // math.isqrt(standing ** lean) + 1 for standing in range(2, count + 1)]
    surplus, given = total - limit - (count - 1), [1] * (count - 1)
    while surplus > 0:
        movable = [i for i in range(count - 1) if given[i] < limit]
        pool, remaining = sum([weights[i] for i in movable]), surplus
        for i in movable:
            addition = min(limit - given[i], max(1, remaining * weights[i] // pool), surplus)
            given[i] = given[i] + addition
            surplus = surplus - addition
    return np.array([limit] + given)


def uneven(own_key, count, total, most, skew):
    if count == 2:
        one = jax.random.randint(own_key, (), max(1, total - most), min(most, total - 1) + 1)
        return jnp.stack([one, total - one])
    sizes = jnp.asarray(length_profile(count, total, most, skew), jnp.int32)
    couples = (count - 1) // 2
    giver, taker = sizes[1:1 + 2 * couples:2], sizes[2:2 + 2 * couples:2]
    room = jnp.minimum(giver - 1, most - taker)
    moved = jax.random.randint(jax.random.fold_in(own_key, 1), (couples,), 0, 1 << 20) % (room + 1)
    sizes = sizes.at[1:1 + 2 * couples:2].set(giver - moved).at[2:2 + 2 * couples:2].set(taker + moved)
    return sizes[jax.random.permutation(jax.random.fold_in(own_key, 2), count)]


def noise(key, shape, scale, reach, cuts=(), kind=jnp.bfloat16):
    values = jax.random.normal(key, shape, jnp.float32) * scale
    if len(cuts) > 0:
        values = steps_of(key, shape, cuts, -0.22, 0.18) * values
    return jnp.clip(values, min=-reach, max=reach).astype(kind)


def heavy_noise(own_key, extent, scale, bound, pieces, heavy, held_as=jnp.bfloat16):
    values = scale * jax.random.normal(own_key, extent, jnp.float32)
    if pieces:
        values = values * steps_of(own_key, extent, pieces, -0.22, 0.18)
    return jnp.clip(with_spikes(values, jax.random.fold_in(own_key, 3), *heavy), -bound, bound).astype(held_as)


def setup_inputs(seed: int = 0) -> dict:
    key_list = jax.random.split(jax.random.key(seed), 7)
    hidden = heavy_noise(key_list[0], (SPAN_COUNT, SPAN_TOKENS, D), 1.0, 6.0, ((0, 16), (1, 16)), (0, 2, 16, 2.0))
    queries = draw_queries(jax.random.fold_in(key_list[6], 71), 0)
    keys = draw_keys(jax.random.fold_in(key_list[6], 71), 0)
    value_weight = noise(key_list[3], (D, KW), D ** -0.5, 0.078125, ((0, 16),))
    doc_ids = jax.vmap(lambda own: jnp.searchsorted(jnp.cumsum(uneven(own, 4, SPAN_TOKENS, SPAN_TOKENS // 2, 2)), jnp.arange(SPAN_TOKENS), side="right"))(jax.random.split(key_list[4], SPAN_COUNT)).reshape((SPAN_COUNT, SPAN_TOKENS)).astype(jnp.int32)
    cotangent = noise(key_list[5], (SPAN_COUNT, SPAN_TOKENS, QW), 1.0, 6.0, ((0, 16), (1, 16)))
    return {"hidden": hidden, "queries": queries, "keys": keys, "value_weight": value_weight, "doc_ids": doc_ids, "cotangent": cotangent}


def attend_span(operands):
    query_gathered, key_gathered, value_gathered, doc, gradient_total = operands
    scale = HEAD_SIZE ** -0.5

    def key_slices(key_tile):
        start_offset = (key_tile * TOKENS_PER_SLOT).astype(jnp.int32)
        key_head_rows = lax.dynamic_slice_in_dim(key_gathered, start_offset, TOKENS_PER_SLOT, 0).reshape(TOKENS_PER_SLOT, KEY_VALUE_HEADS, HEAD_SIZE).astype(jnp.float32)
        value_head_rows = lax.dynamic_slice_in_dim(value_gathered, start_offset, TOKENS_PER_SLOT, 0).reshape(TOKENS_PER_SLOT, KEY_VALUE_HEADS, HEAD_SIZE).astype(jnp.float32)
        key_doc = lax.dynamic_slice_in_dim(doc, start_offset, TOKENS_PER_SLOT, 0)
        key_pos = start_offset + jnp.arange(TOKENS_PER_SLOT, dtype=jnp.int32)
        return start_offset, key_head_rows, value_head_rows, key_doc, key_pos

    def query_step(carry, query_block):
        key_gradient_sum, value_gradient_sum = carry
        query_offset = (query_block * TOKENS_PER_SLOT).astype(jnp.int32)
        query_head_rows = lax.dynamic_slice_in_dim(query_gathered, query_offset, TOKENS_PER_SLOT, 0).reshape(TOKENS_PER_SLOT, KEY_VALUE_HEADS, QUERY_PER_KV, HEAD_SIZE).astype(jnp.float32)
        gradient_heads = lax.dynamic_slice_in_dim(gradient_total, query_offset, TOKENS_PER_SLOT, 0).reshape(TOKENS_PER_SLOT, KEY_VALUE_HEADS, QUERY_PER_KV, HEAD_SIZE).astype(jnp.float32)
        query_doc = lax.dynamic_slice_in_dim(doc, query_offset, TOKENS_PER_SLOT, 0)
        query_pos = query_offset + jnp.arange(TOKENS_PER_SLOT, dtype=jnp.int32)

        def masked_scores(key_head_rows, key_doc, key_pos):
            scores = jnp.einsum('qhgd,khd->hgqk', query_head_rows, key_head_rows) * scale
            allow = (key_pos[None, :] <= query_pos[:, None]) & (key_doc[None, :] == query_doc[:, None])
            return jnp.where(allow, scores, -1e30), allow

        def forward_step(state, key_tile):
            peak, total, accum = state
            start_offset, key_head_rows, value_head_rows, key_doc, key_pos = key_slices(key_tile)
            masked, allow = masked_scores(key_head_rows, key_doc, key_pos)
            new_peak = jnp.maximum(peak, jnp.max(masked, axis=-1))
            expd = jnp.where(allow, jnp.exp(masked - new_peak[..., None]), 0.0)
            factor = jnp.exp(peak - new_peak)
            weights = lax.optimization_barrier(expd.astype(jnp.bfloat16)).astype(jnp.float32)
            total = total * factor + jnp.sum(expd, axis=-1)
            accum = accum * factor[..., None] + jnp.einsum('hgqk,khd->hgqd', weights, value_head_rows)
            return (new_peak, total, accum), None

        head_layout = (KEY_VALUE_HEADS, QUERY_PER_KV, TOKENS_PER_SLOT)
        start_state = (jnp.full(head_layout, -1e30, jnp.float32), jnp.zeros(head_layout, jnp.float32),
                       jnp.zeros((KEY_VALUE_HEADS, QUERY_PER_KV, TOKENS_PER_SLOT, HEAD_SIZE), jnp.float32))
        (peak, total, accum), unused = lax.scan(forward_step, start_state, jnp.arange(N_SEQ, dtype=jnp.int32))
        out_heads = (accum / total[..., None]).astype(jnp.bfloat16).transpose(2, 0, 1, 3)
        delta = jnp.sum(gradient_heads * out_heads.astype(jnp.float32), axis=-1).transpose(1, 2, 0)

        def backward_step(state, key_tile):
            grad_query, key_total, value_total = state
            start_offset, key_head_rows, value_head_rows, key_doc, key_pos = key_slices(key_tile)
            masked, allow = masked_scores(key_head_rows, key_doc, key_pos)
            probs = jnp.where(allow, jnp.exp(masked - peak[..., None]), 0.0) / total[..., None]
            probs_b = lax.optimization_barrier(probs.astype(jnp.bfloat16)).astype(jnp.float32)
            dprob = jnp.einsum('qhgd,khd->hgqk', gradient_heads, value_head_rows)
            dscore = lax.optimization_barrier((probs * (dprob - delta[..., None])).astype(jnp.bfloat16)).astype(jnp.float32)
            grad_query = grad_query + jnp.einsum('hgqk,khd->qhgd', dscore, key_head_rows)
            key_part = lax.optimization_barrier((jnp.einsum('hgqk,qhgd->khd', dscore, query_head_rows) * scale).astype(jnp.bfloat16)).astype(jnp.float32)
            value_part = lax.optimization_barrier(jnp.einsum('hgqk,qhgd->khd', probs_b, gradient_heads).astype(jnp.bfloat16)).astype(jnp.float32)
            key_total = lax.dynamic_update_slice_in_dim(key_total, lax.dynamic_slice_in_dim(key_total, start_offset, TOKENS_PER_SLOT, 0) + key_part, start_offset, 0)
            value_total = lax.dynamic_update_slice_in_dim(value_total, lax.dynamic_slice_in_dim(value_total, start_offset, TOKENS_PER_SLOT, 0) + value_part, start_offset, 0)
            return (grad_query, key_total, value_total), None

        reverse_state = (jnp.zeros((TOKENS_PER_SLOT, KEY_VALUE_HEADS, QUERY_PER_KV, HEAD_SIZE), jnp.float32), key_gradient_sum, value_gradient_sum)
        (grad_query, key_gradient_sum, value_gradient_sum), unused = lax.scan(backward_step, reverse_state, jnp.arange(N_SEQ, dtype=jnp.int32))
        grad_rows = (grad_query * scale).astype(jnp.bfloat16)
        return (key_gradient_sum, value_gradient_sum), (out_heads.reshape(TOKENS_PER_SLOT, QW), grad_rows.reshape(TOKENS_PER_SLOT, QW))

    zero_filled = jnp.zeros((SPAN_TOKENS, KEY_VALUE_HEADS, HEAD_SIZE), jnp.float32)
    (key_gradient_sum, value_gradient_sum), (outs, grads) = lax.scan(query_step, (zero_filled, zero_filled), jnp.arange(N_SEQ, dtype=jnp.int32))
    return (outs.reshape(SPAN_TOKENS, QW), grads.reshape(SPAN_TOKENS, QW),
            key_gradient_sum.reshape(SPAN_TOKENS, KW).astype(jnp.bfloat16), value_gradient_sum.reshape(SPAN_TOKENS, KW).astype(jnp.bfloat16))


def reference(hidden, queries, keys, value_weight, doc_ids, cotangent):
    flat = hidden.reshape(SPAN_COUNT * SPAN_TOKENS, D)
    values = jnp.dot(flat, value_weight, preferred_element_type=jnp.float32).astype(jnp.bfloat16).reshape(SPAN_COUNT, SPAN_TOKENS, KW)
    attn_out, grad_queries, grad_keys, grad_values = lax.map(attend_span, (queries, keys, values, doc_ids, cotangent))
    grad_flat = grad_values.reshape(SPAN_COUNT * SPAN_TOKENS, KW)
    grad_hidden = jnp.dot(grad_flat, value_weight.T, preferred_element_type=jnp.float32).astype(jnp.bfloat16).reshape(SPAN_COUNT, SPAN_TOKENS, D)
    grad_weight = jnp.dot(flat.T, grad_flat, preferred_element_type=jnp.float32)
    return attn_out, grad_queries, grad_keys, grad_hidden, grad_weight
```

```python
import functools
import jax
import jax.numpy as jnp
from jax import lax
from jax.experimental import pallas as pl
from jax.experimental.pallas import tpu as pltpu
from jax.sharding import PartitionSpec as P

HS = 128
G = 5
BLK = 128
WIN = 9 * BLK
CC = HS ** -0.5 * 1.4426950408889634
SCALE = HS ** -0.5

def dott(a, b, ca, cb):
    return lax.dot_general(a, b, (((ca,), (cb,)), ((), ())), preferred_element_type=jnp.float32)

def attn_kernel(nkv, nt, q_ref, k_ref, v_ref, cot_ref, qd_ref, kd_ref, o_ref, dq_ref, dkv_ref,
                bias_ref, eb_ref, ds_ref, dob_ref, qs_ref, dk_acc, dv_acc):
    for t in range(nt):
        allow = qd_ref[t * BLK:(t + 1) * BLK, :] == kd_ref[:, t * BLK:t * BLK + WIN]
        r = lax.broadcasted_iota(jnp.int32, (BLK, WIN), 0)
        c = lax.broadcasted_iota(jnp.int32, (BLK, WIN), 1)
        allow = allow & (c - (WIN - BLK) <= r)
        bias_ref[t * BLK:(t + 1) * BLK, :] = jnp.where(allow, 0.0, -1e30)

    def head(g, _):
        gc = pl.multiple_of(g * HS, HS)
        dk_acc[...] = jnp.zeros_like(dk_acc)
        dv_acc[...] = jnp.zeros_like(dv_acc)
        for t in range(nt):
            rows = pl.ds(t * BLK, BLK)
            win = pl.ds(t * BLK, WIN)
            k = k_ref[win, pl.ds(gc, HS)]
            v = v_ref[win, pl.ds(gc, HS)]
            for h in range(G):
                col = pl.ds(pl.multiple_of(g * (G * HS) + h * HS, HS), HS)
                hr = pl.ds(h * BLK, BLK)
                q = q_ref[rows, col]
                s = dott(q, k, 1, 1) + bias_ref[rows, :]
                m = jnp.max(s, axis=1, keepdims=True)
                e = jnp.exp2((s - m) * CC)
                l = jnp.sum(e, axis=1, keepdims=True)
                eb = e.astype(jnp.bfloat16)
                inv = 1.0 / l
                ob = (dott(eb, v, 1, 0) * inv).astype(jnp.bfloat16)
                o_ref[rows, col] = ob
                do = cot_ref[rows, col].astype(jnp.float32)
                delta = jnp.sum(do * ob.astype(jnp.float32), axis=1, keepdims=True) * inv
                dob = (do * inv).astype(jnp.bfloat16)
                dp = dott(dob, v, 1, 1)
                ds = (e * (dp - delta)).astype(jnp.bfloat16)
                dq_ref[rows, col] = (dott(ds, k, 1, 0) * SCALE).astype(jnp.bfloat16)
                eb_ref[hr, :] = eb
                ds_ref[hr, :] = ds
                dob_ref[hr, :] = dob
                qs_ref[hr, :] = q
            dk_acc[win, :] += dott(ds_ref[...], qs_ref[...], 0, 0)
            dv_acc[win, :] += dott(eb_ref[...], dob_ref[...], 0, 0)
        dkv_ref[:, pl.ds(gc, HS)] = (dk_acc[...] * SCALE).astype(jnp.bfloat16)
        dkv_ref[:, pl.ds(pl.multiple_of(nkv * HS + g * HS, HS), HS)] = dv_acc[...].astype(jnp.bfloat16)
        return 0

    lax.fori_loop(0, nkv, head, 0)

def attention(q, k, v, cot, qd, kd, nkv, nt):
    rows = (nt + 8) * BLK
    shp = jax.ShapeDtypeStruct
    vm = pl.BlockSpec(memory_space=pltpu.VMEM)
    return pl.pallas_call(
        functools.partial(attn_kernel, nkv, nt),
        out_shape=(shp(q.shape, jnp.bfloat16), shp(q.shape, jnp.bfloat16), shp((rows, 2 * nkv * HS), jnp.bfloat16)),
        in_specs=[vm] * 6, out_specs=(vm,) * 3,
        scratch_shapes=[
            pltpu.VMEM((nt * BLK, WIN), jnp.float32),
            pltpu.VMEM((G * BLK, WIN), jnp.bfloat16),
            pltpu.VMEM((G * BLK, WIN), jnp.bfloat16),
            pltpu.VMEM((G * BLK, HS), jnp.bfloat16),
            pltpu.VMEM((G * BLK, HS), jnp.bfloat16),
            pltpu.VMEM((rows, HS), jnp.float32),
            pltpu.VMEM((rows, HS), jnp.float32),
        ],
        compiler_params=pltpu.CompilerParams(vmem_limit_bytes=24 << 20),
        name="attention",
    )(q, k, v, cot, qd, kd)


MESH = pl.DeviceIdType.MESH
BF = jnp.bfloat16
F32 = jnp.float32


def rcopy(src, dst, ssem, rsem, dev):
    return pltpu.make_async_remote_copy(
        src_ref=src, dst_ref=dst, send_sem=ssem, recv_sem=rsem, device_id=dev, device_id_type=MESH
    )


def mo(v, n):
    return pl.multiple_of(v, n)


class Where:
    def __init__(self):
        a, s = lax.axis_index("dp"), lax.axis_index("seq")
        self.a, self.s = a, s
        self.zl, self.x = a // 4, lax.rem(a, 4)
        self.core, self.c = lax.rem(s, 2), s // 2
        self.y, self.zh = self.c // 2, lax.rem(self.c, 2)
        self.other = 1 - self.core
        self.partner = (a, self.c * 2 + self.other)
        self.xp, self.xm = self.at_x(1), self.at_x(3)
        self.zp, self.zm = self.at_z(1), self.at_z(7)

    def at_x(self, d):
        return (self.zl * 4 + lax.rem(self.x + d, 4), self.s)

    def at_z(self, d):
        z = lax.rem(self.zh * 4 + self.zl + d, 8)
        return (lax.rem(z, 4) * 4 + self.x, (self.y * 2 + z // 4) * 2 + self.core)

    def chip(self, c):
        return (self.a, c * 2 + self.core)

    def enter(self):
        barrier = pltpu.get_barrier_semaphore()
        peers = [self.partner, self.xp, self.xm, self.zp, self.zm]
        peers += [self.chip(lax.rem(self.c + d, 8)) for d in range(1, 8)]
        for p in peers:
            pl.semaphore_signal(barrier, inc=1, device_id=p, device_id_type=MESH)
        pl.semaphore_wait(barrier, len(peers))


class Gather4:
    def __init__(self, blk, h0, h1, i, p, m, ss, rs):
        one, two, three = lax.rem(i + 1, 4), lax.rem(i + 2, 4), lax.rem(i + 3, 4)
        self.first = [rcopy(blk(i), blk(i), ss.at[0], rs.at[0], p), rcopy(blk(i), blk(i), ss.at[1], rs.at[1], m)]
        self.first_in = [rcopy(blk(three), blk(three), ss.at[0], rs.at[0], p), rcopy(blk(one), blk(one), ss.at[1], rs.at[1], m)]
        self.second = [rcopy(h0(three), h0(three), ss.at[2], rs.at[2], p), rcopy(h1(one), h1(one), ss.at[3], rs.at[3], m)]
        self.second_in = [rcopy(h0(two), h0(two), ss.at[2], rs.at[2], p), rcopy(h1(two), h1(two), ss.at[3], rs.at[3], m)]

    def start(self):
        for r in self.first:
            r.start()

    def relay(self):
        for got, go in zip(self.first_in, self.second):
            got.wait_recv()
            go.start()

    def finish(self):
        for r in self.second_in:
            r.wait_recv()

    def drain(self):
        for r in self.first + self.second:
            r.wait_send()


class Scatter4:
    def __init__(self, ref, at, h0, h1, i, p, m, halves, wholes, ss, rs):
        self.ref, self.at, self.h0, self.h1, self.i = ref, at, h0, h1, i
        self.halves, self.wholes = halves, wholes
        one, two, three = lax.rem(i + 1, 4), lax.rem(i + 2, 4), lax.rem(i + 3, 4)
        self.one, self.three = one, three
        self.first = [
            rcopy(ref.at[h0(two)], halves.at[0], ss.at[0], rs.at[0], p),
            rcopy(ref.at[h1(two)], halves.at[1], ss.at[1], rs.at[1], m),
        ]
        self.second = [
            rcopy(ref.at[at(one)], wholes.at[0], ss.at[2], rs.at[2], p),
            rcopy(ref.at[at(three)], wholes.at[1], ss.at[3], rs.at[3], m),
        ]

    def start(self):
        for r in self.first:
            r.start()

    def relay(self):
        for n, where in ((0, self.h0(self.one)), (1, self.h1(self.three))):
            self.first[n].wait_recv()
            self.ref[where] = (self.ref[where].astype(F32) + self.halves[n].astype(F32)).astype(BF)
            self.second[n].start()

    def finish(self):
        for r in self.second:
            r.wait_recv()
        own = self.at(self.i)
        self.ref[own] = (
            self.ref[own].astype(F32) + self.wholes[0].astype(F32) + self.wholes[1].astype(F32)
        ).astype(BF)

    def drain(self):
        for r in self.first + self.second:
            r.wait_send()


def gather_kernel(w, hid, q, cot, k, docs, wh, hid2, q2, cot2, kw, vw, dw, vacc, wss, wrs, pss, prs, lsem, kss, krs):
    me = Where()
    c = me.c
    me.enter()
    qcol = lambda n: pl.ds(mo(n * 1280, 128), 1280)
    kcol = lambda n: pl.ds(mo(n * 256, 128), 256)
    local = [
        (w.at[:, kcol(me.core)], wh.at[me.zl, me.x]),
        (k.at[:, kcol(me.core)], kw.at[4, me.core]),
        (docs, dw.at[4, me.core]),
        (hid, hid2.at[me.core]),
        (q.at[:, qcol(me.core)], q2.at[me.core]),
        (cot.at[:, qcol(me.core)], cot2.at[me.core]),
    ]
    local = [pltpu.make_async_copy(s, d, lsem.at[n]) for n, (s, d) in enumerate(local)]
    for r in local:
        r.start()
    swap = [
        (k.at[:, kcol(me.other)], kw.at[4, me.core], kw.at[4, me.other]),
        (docs, dw.at[4, me.core], dw.at[4, me.other]),
        (hid, hid2.at[me.core], hid2.at[me.other]),
        (q.at[:, qcol(me.other)], q2.at[me.core], q2.at[me.other]),
        (cot.at[:, qcol(me.other)], cot2.at[me.core], cot2.at[me.other]),
    ]
    swap_in = [rcopy(s, i, pss.at[n], prs.at[n], me.partner) for n, (s, d, i) in enumerate(swap)]
    swap = [rcopy(s, d, pss.at[n], prs.at[n], me.partner) for n, (s, d, i) in enumerate(swap)]
    for r in swap:
        r.start()

    ra, rb = pl.ds(0, 160), pl.ds(160, 160)
    a0, a1, b0, b1 = pl.ds(0, 80), pl.ds(80, 80), pl.ds(160, 80), pl.ds(240, 80)
    ga1 = Gather4(*[lambda j, r=r: wh.at[me.zl, j, r] for r in (ra, a0, a1)], me.x, me.xp, me.xm, wss.at[0], wrs.at[0])
    gb1 = Gather4(*[lambda j, r=r: wh.at[j, me.x, r] for r in (rb, b0, b1)], me.zl, me.zp, me.zm, wss.at[1], wrs.at[1])
    ga2 = Gather4(*[lambda j, r=r: wh.at[j, :, r] for r in (ra, a0, a1)], me.zl, me.zp, me.zm, wss.at[2], wrs.at[2])
    gb2 = Gather4(*[lambda j, r=r: wh.at[:, j, r] for r in (rb, b0, b1)], me.x, me.xp, me.xm, wss.at[3], wrs.at[3])
    local[0].wait()
    ga1.start()
    gb1.start()

    def spread(buf, n):
        return [rcopy(buf.at[4], buf.at[4 - d], kss.at[n, d - 1], krs.at[n, 4 - d], me.chip(lax.rem(c + d, 8))) for d in range(1, 5)]

    def spread_in(buf, n):
        return [rcopy(buf.at[4], buf.at[j], kss.at[n, 0], krs.at[n, j], me.chip(lax.rem(c + 4 + j, 8))) for j in range(4)]

    def start_spread(sends):
        for d, r in enumerate(sends):
            @pl.when(c + d + 1 < 8)
            def _():
                r.start()

    for j in range(4):
        @pl.when(c < 4 - j)
        def _():
            kw[j] = jnp.zeros(kw.shape[1:], BF)
            vw[j] = jnp.zeros(vw.shape[1:], BF)
            dw[j] = jnp.full(dw.shape[1:], -1, jnp.int32)

    local[1].wait()
    local[2].wait()
    swap_in[0].wait_recv()
    swap_in[1].wait_recv()
    ks, ds, vs = spread(kw, 0), spread(dw, 1), spread(vw, 2)
    start_spread(ks)
    start_spread(ds)
    ga1.relay()
    gb1.relay()
    ga1.finish()
    ga2.start()
    gb1.finish()
    gb2.start()
    ga2.relay()
    gb2.relay()
    for r in local[3:]:
        r.wait()
    for r in swap_in[2:]:
        r.wait_recv()
    ga2.finish()
    gb2.finish()
    for z in range(4):
        h = hid2[:, :, z * 1280:(z + 1) * 1280].reshape(256, 1280)
        part = jnp.dot(h, wh[z].reshape(1280, 256), preferred_element_type=F32)
        vacc[...] = part if z == 0 else vacc[...] + part
    vw[4] = vacc[...].astype(BF).reshape(2, 128, 256)
    start_spread(vs)
    for n, (buf, sends) in enumerate(((kw, ks), (dw, ds), (vw, vs))):
        for j, r in enumerate(spread_in(buf, n)):
            @pl.when(c >= 4 - j)
            def _():
                r.wait_recv()
        for d, r in enumerate(sends):
            @pl.when(c + d + 1 < 8)
            def _():
                r.wait_send()
    for r in swap:
        r.wait_send()
    for g in (ga1, gb1, ga2, gb2):
        g.drain()


def gather(w, hid, q, cot, k, docs):
    shp = jax.ShapeDtypeStruct
    vm = pl.BlockSpec(memory_space=pltpu.VMEM)
    dma = pltpu.SemaphoreType.DMA
    return pl.pallas_call(
        gather_kernel,
        out_shape=(
            shp((4, 4, 320, 256), BF), shp((2, 128, 5120), BF), shp((2, 128, 1280), BF), shp((2, 128, 1280), BF),
            shp((5, 2, 128, 256), BF), shp((5, 2, 128, 256), BF), shp((5, 2, 8, 128), jnp.int32),
        ),
        in_specs=[vm] * 6,
        out_specs=(vm,) * 7,
        scratch_shapes=[
            pltpu.VMEM((256, 256), F32),
            dma((4, 4)), dma((4, 4)), dma((5,)), dma((5,)), dma((6,)), dma((3, 4)), dma((3, 4)),
        ],
        compiler_params=pltpu.CompilerParams(collective_id=0, has_side_effects=True, vmem_limit_bytes=28 << 20),
        name="gather",
    )(w, hid, q, cot, k, docs)


def reduce_kernel(dkv, o2, dq2, hid2, wh, attn, gq, gk, gh, gw, rb, acc, gkv, gvs, ghp, ghr, gho, dw, halves, wholes, halves2, wholes2,
                  yr, zs, zr, fin, pr, wss, wrs, pss, prs, lsem, kss, krs, yss, yrs):
    me = Where()
    c = me.c
    me.enter()
    sends = [rcopy(dkv.at[j], rb.at[j], kss.at[j], krs.at[j], me.chip(lax.rem(c + 4 + j, 8))) for j in range(4)]
    for j, r in enumerate(sends):
        @pl.when(c >= 4 - j)
        def _():
            r.start()
    qcol = lambda n: pl.ds(mo(n * 1280, 128), 1280)
    kcol = lambda n: pl.ds(mo(n * 256, 128), 256)
    local = [(o2.at[me.core], attn.at[:, qcol(me.core)]), (dq2.at[me.core], gq.at[:, qcol(me.core)])]
    local = [pltpu.make_async_copy(s, d, lsem.at[n]) for n, (s, d) in enumerate(local)]
    swap = [
        rcopy(o2.at[me.other], attn.at[:, qcol(me.core)], pss.at[0], prs.at[0], me.partner),
        rcopy(dq2.at[me.other], gq.at[:, qcol(me.core)], pss.at[1], prs.at[1], me.partner),
    ]
    swap_in = [
        rcopy(o2.at[me.other], attn.at[:, qcol(me.other)], pss.at[0], prs.at[0], me.partner),
        rcopy(dq2.at[me.other], gq.at[:, qcol(me.other)], pss.at[1], prs.at[1], me.partner),
    ]
    for r in local + swap:
        r.start()
    acc[...] = dkv[4].astype(F32)
    for j in range(3, -1, -1):
        @pl.when(c + 4 - j < 8)
        def _():
            rcopy(dkv.at[j], rb.at[j], kss.at[j], krs.at[j], me.chip(lax.rem(c + 4 - j, 8))).wait_recv()
            acc[...] += rb[j].astype(F32)
    gkv[...] = acc[:, :256].astype(BF).reshape(2, 128, 256)
    gvs[...] = acc[:, 256:].astype(BF).reshape(2, 128, 256)
    gv = gvs[...].reshape(256, 256)
    for z in range(4):
        h = hid2[:, :, z * 1280:(z + 1) * 1280].reshape(256, 1280)
        dw[z] = dott(h, gv, 0, 0).astype(BF).reshape(4, 320, 256)

    a0, a1, b0, b1 = pl.ds(0, 80), pl.ds(80, 80), pl.ds(160, 80), pl.ds(240, 80)
    ra, rb_ = pl.ds(0, 160), pl.ds(160, 160)
    sa1 = Scatter4(dw, *[lambda j, r=r: (j, slice(None), r) for r in (ra, a0, a1)], me.zl, me.zp, me.zm,
                   halves.at[0], wholes.at[0], wss.at[0], wrs.at[0])
    sb1 = Scatter4(dw, *[lambda j, r=r: (slice(None), j, r) for r in (rb_, b0, b1)], me.x, me.xp, me.xm,
                   halves.at[1], wholes.at[1], wss.at[1], wrs.at[1])
    sa2 = Scatter4(dw, *[lambda j, r=r: (me.zl, j, r) for r in (ra, a0, a1)], me.x, me.xp, me.xm,
                   halves2.at[0], wholes2.at[0], wss.at[2], wrs.at[2])
    sb2 = Scatter4(dw, *[lambda j, r=r: (j, me.x, r) for r in (rb_, b0, b1)], me.zl, me.zp, me.zm,
                   halves2.at[1], wholes2.at[1], wss.at[3], wrs.at[3])
    sa1.start()
    sb1.start()
    swap.append(rcopy(gkv.at[me.other], gk.at[:, kcol(me.core)], pss.at[2], prs.at[2], me.partner))
    swap_in.append(rcopy(gkv.at[me.other], gk.at[:, kcol(me.other)], pss.at[2], prs.at[2], me.partner))
    local.append(pltpu.make_async_copy(gkv.at[me.core], gk.at[:, kcol(me.core)], lsem.at[2]))
    swap[2].start()
    local[2].start()
    for z in range(4):
        cols = slice(z * 1280, (z + 1) * 1280)
        ghp[:, cols] = dott(gvs[me.other], wh[z].reshape(1280, 256), 1, 1).astype(BF)
    swap.append(rcopy(ghp, ghr, pss.at[3], prs.at[3], me.partner))
    swap_in.append(swap[3])
    swap[3].start()
    sa1.relay()
    sb1.relay()
    for z in range(4):
        cols = slice(z * 1280, (z + 1) * 1280)
        gho[:, cols] = dott(gvs[me.core], wh[z].reshape(1280, 256), 1, 1)
    sa1.finish()
    sa2.start()
    sb1.finish()
    sb2.start()
    swap_in[3].wait_recv()
    gh[...] = (gho[...] + ghr[...].astype(F32)).astype(BF)
    sa2.relay()
    sb2.relay()
    sa2.finish()
    sb2.finish()

    piece = lambda j: dw.at[me.zl, me.x, pl.ds(mo(j * 80, 16), 80)]
    ychip = lambda d: me.chip(lax.rem(me.y + d, 4) * 2 + me.zh)
    ysend = [rcopy(piece(lax.rem(me.y + d, 4)), yr.at[d - 1], yss.at[d - 1], yrs.at[d - 1], ychip(d)) for d in range(1, 4)]
    for r in ysend:
        r.start()
    tot = dw[me.zl, me.x, pl.ds(mo(me.y * 80, 16), 80)].astype(F32)
    for d in range(3):
        ysend[d].wait_recv()
        tot = tot + yr[d].astype(F32)
    zs[...] = tot.astype(BF)
    zx = rcopy(zs, zr, yss.at[3], yrs.at[3], me.chip(me.y * 2 + 1 - me.zh))
    zx.start()
    zx.wait_recv()
    fin[me.y] = (zs[...].astype(F32) + zr[...].astype(F32)).astype(BF)
    ysend2 = [rcopy(fin.at[me.y], fin.at[me.y], yss.at[3 + d], yrs.at[3 + d], ychip(d)) for d in range(1, 4)]
    for r in ysend2:
        r.start()
    for d in range(1, 4):
        src = fin.at[lax.rem(me.y + 4 - d, 4)]
        rcopy(src, src, yss.at[3 + d], yrs.at[3 + d], ychip(d)).wait_recv()
    swap.append(rcopy(fin, pr, pss.at[4], prs.at[4], me.partner))
    swap_in.append(swap[4])
    swap[4].start()
    gw[:, kcol(me.core)] = fin[...].astype(F32).reshape(320, 256)
    swap_in[4].wait_recv()
    gw[:, kcol(me.other)] = pr[...].astype(F32).reshape(320, 256)
    for r in local:
        r.wait()
    for r in swap_in[:3]:
        r.wait_recv()
    for r in swap + ysend + ysend2 + [zx]:
        r.wait_send()
    for j, r in enumerate(sends):
        @pl.when(c >= 4 - j)
        def _():
            r.wait_send()
    for g in (sa1, sb1, sa2, sb2):
        g.drain()


def reduce_all(dkv, o2, dq2, hid2, wh):
    shp = jax.ShapeDtypeStruct
    vm = pl.BlockSpec(memory_space=pltpu.VMEM)
    dma = pltpu.SemaphoreType.DMA
    v = pltpu.VMEM
    return pl.pallas_call(
        reduce_kernel,
        out_shape=(
            shp((128, 2560), BF), shp((128, 2560), BF), shp((128, 512), BF), shp((128, 5120), BF), shp((320, 512), F32),
        ),
        in_specs=[vm] * 5,
        out_specs=(vm,) * 5,
        scratch_shapes=[
            v((4, 256, 512), BF), v((256, 512), F32), v((2, 128, 256), BF), v((2, 128, 256), BF),
            v((128, 5120), BF), v((128, 5120), BF), v((128, 5120), F32), v((4, 4, 320, 256), BF),
            v((2, 2, 4, 80, 256), BF), v((2, 2, 4, 160, 256), BF), v((2, 2, 80, 256), BF), v((2, 2, 160, 256), BF),
            v((3, 80, 256), BF), v((80, 256), BF), v((80, 256), BF), v((4, 80, 256), BF), v((4, 80, 256), BF),
            dma((4, 4)), dma((4, 4)), dma((5,)), dma((5,)), dma((3,)), dma((4,)), dma((4,)), dma((7,)), dma((7,)),
        ],
        compiler_params=pltpu.CompilerParams(collective_id=1, has_side_effects=True, vmem_limit_bytes=32 << 20),
        name="reduce",
    )(dkv, o2, dq2, hid2, wh)


def body(hidden, queries, keys, value_weight, doc_ids, cotangent):
    docs = jnp.broadcast_to(doc_ids, (8, BLK))
    wh, hid2, q2, cot2, kw, vw, dw = gather(value_weight, hidden[0], queries[0], cotangent[0], keys[0], docs)
    kd = dw[:, :, 0, :].reshape(1, 1280)
    qd = kd[:, 1024:].reshape(256, 1)
    o2, dq2, dkv = attention(
        q2.reshape(256, 1280), kw.reshape(1280, 256), vw.reshape(1280, 256), cot2.reshape(256, 1280), qd, kd, 2, 2
    )
    attn, gq, gk, gh, gw = reduce_all(
        dkv.reshape(5, 256, 512), o2.reshape(2, 128, 1280), dq2.reshape(2, 128, 1280), hid2, wh
    )
    return attn[None], gq[None], gk[None], gh[None], gw


def solution(mesh):
    rows = P("dp", "seq", None)
    return jax.shard_map(
        body, mesh=mesh,
        in_specs=(rows, rows, rows, P("dp", None), P("dp", "seq"), rows),
        out_specs=(rows, rows, rows, rows, P("dp", None)),
        check_vma=False,
    )
```

```python
import jax
import jax.numpy as jnp
from jax import lax
from jax.experimental import pallas as pl
from jax.experimental.pallas import tpu as pltpu
from jax.sharding import PartitionSpec as P

HS = 128
G = 5
BLK = 128
WIN = 9 * BLK
CC = HS ** -0.5 * 1.4426950408889634
SCALE = HS ** -0.5

def dott(a, b, ca, cb):
    return lax.dot_general(a, b, (((ca,), (cb,)), ((), ())), preferred_element_type=jnp.float32)

MESH = pl.DeviceIdType.MESH
BF = jnp.bfloat16
F32 = jnp.float32


def rcopy(src, dst, ssem, rsem, dev):
    return pltpu.make_async_remote_copy(
        src_ref=src, dst_ref=dst, send_sem=ssem, recv_sem=rsem, device_id=dev, device_id_type=MESH
    )


def mo(v, n):
    return pl.multiple_of(v, n)


class Where:
    def __init__(self):
        a, s = lax.axis_index("dp"), lax.axis_index("seq")
        self.a, self.s = a, s
        self.zl, self.x = a // 4, lax.rem(a, 4)
        self.core, self.c = lax.rem(s, 2), s // 2
        self.y, self.zh = self.c // 2, lax.rem(self.c, 2)
        self.other = 1 - self.core
        self.partner = (a, self.c * 2 + self.other)
        self.xp, self.xm = self.at_x(1), self.at_x(3)
        self.zp, self.zm = self.at_z(1), self.at_z(7)

    def at_x(self, d):
        return (self.zl * 4 + lax.rem(self.x + d, 4), self.s)

    def at_z(self, d):
        z = lax.rem(self.zh * 4 + self.zl + d, 8)
        return (lax.rem(z, 4) * 4 + self.x, (self.y * 2 + z // 4) * 2 + self.core)

    def chip(self, c):
        return (self.a, c * 2 + self.core)

    def enter(self):
        barrier = pltpu.get_barrier_semaphore()
        peers = [self.partner, self.xp, self.xm, self.zp, self.zm]
        peers += [self.chip(lax.rem(self.c + d, 8)) for d in range(1, 8)]
        for p in peers:
            pl.semaphore_signal(barrier, inc=1, device_id=p, device_id_type=MESH)
        pl.semaphore_wait(barrier, len(peers))


class Gather4:
    def __init__(self, blk, h0, h1, i, p, m, ss, rs):
        one, two, three = lax.rem(i + 1, 4), lax.rem(i + 2, 4), lax.rem(i + 3, 4)
        self.first = [rcopy(blk(i), blk(i), ss.at[0], rs.at[0], p), rcopy(blk(i), blk(i), ss.at[1], rs.at[1], m)]
        self.first_in = [rcopy(blk(three), blk(three), ss.at[0], rs.at[0], p), rcopy(blk(one), blk(one), ss.at[1], rs.at[1], m)]
        self.second = [rcopy(h0(three), h0(three), ss.at[2], rs.at[2], p), rcopy(h1(one), h1(one), ss.at[3], rs.at[3], m)]
        self.second_in = [rcopy(h0(two), h0(two), ss.at[2], rs.at[2], p), rcopy(h1(two), h1(two), ss.at[3], rs.at[3], m)]

    def start(self):
        for r in self.first:
            r.start()

    def relay(self):
        for got, go in zip(self.first_in, self.second):
            got.wait_recv()
            go.start()

    def finish(self):
        for r in self.second_in:
            r.wait_recv()

    def drain(self):
        for r in self.first + self.second:
            r.wait_send()


class Scatter4:
    def __init__(self, ref, at, h0, h1, i, p, m, halves, wholes, ss, rs):
        self.ref, self.at, self.h0, self.h1, self.i = ref, at, h0, h1, i
        self.halves, self.wholes = halves, wholes
        one, two, three = lax.rem(i + 1, 4), lax.rem(i + 2, 4), lax.rem(i + 3, 4)
        self.one, self.three = one, three
        self.first = [
            rcopy(ref.at[h0(two)], halves.at[0], ss.at[0], rs.at[0], p),
            rcopy(ref.at[h1(two)], halves.at[1], ss.at[1], rs.at[1], m),
        ]
        self.second = [
            rcopy(ref.at[at(one)], wholes.at[0], ss.at[2], rs.at[2], p),
            rcopy(ref.at[at(three)], wholes.at[1], ss.at[3], rs.at[3], m),
        ]

    def start(self):
        for r in self.first:
            r.start()

    def relay(self):
        for n, where in ((0, self.h0(self.one)), (1, self.h1(self.three))):
            self.first[n].wait_recv()
            self.ref[where] = (self.ref[where].astype(F32) + self.halves[n].astype(F32)).astype(BF)
            self.second[n].start()

    def finish(self):
        for r in self.second:
            r.wait_recv()
        own = self.at(self.i)
        self.ref[own] = (
            self.ref[own].astype(F32) + self.wholes[0].astype(F32) + self.wholes[1].astype(F32)
        ).astype(BF)

    def drain(self):
        for r in self.first + self.second:
            r.wait_send()


HA, HB = 64, 96


def mega_kernel(w, hid, q, cot, k, docs, attn, gq, gk, gh, gw,
                wh, hid2, hidt, q2, cot2, kw, vw, dwin, vacc, bias, eb, ds, dob, qs, inv, dl, acc,
                dvb, rv, dkb, rk, o2, dq2, gkb, gvs, ghp, ghr, gho, dw, ha1, wa1, hb1, wb1, ha2, wa2, hb2, wb2,
                yr, zs, zr, fin, pr, wss, wrs, pss, prs, lsem, kss, krs, gss, grs, rss, rrs, yss, yrs):
    me = Where()
    c = me.c
    qcol = lambda n: pl.ds(mo(n * 1280, 128), 1280)
    kcol = lambda n: pl.ds(mo(n * 256, 128), 256)
    local = [
        (k.at[:, kcol(me.core)], kw.at[4, me.core]),
        (docs, dwin.at[4, me.core]),
        (w.at[:, kcol(me.core)], wh.at[me.zl, me.x]),
        (hid, hid2.at[me.core]),
        (q.at[:, qcol(me.core)], q2.at[me.core]),
        (cot.at[:, qcol(me.core)], cot2.at[me.core]),
    ]
    local = [pltpu.make_async_copy(s, d, lsem.at[n]) for n, (s, d) in enumerate(local)]
    for r in local:
        r.start()
    me.enter()
    swap = [
        (k.at[:, kcol(me.other)], kw.at[4, me.core], kw.at[4, me.other]),
        (docs, dwin.at[4, me.core], dwin.at[4, me.other]),
        (q.at[:, qcol(me.other)], q2.at[me.core], q2.at[me.other]),
        (cot.at[:, qcol(me.other)], cot2.at[me.core], cot2.at[me.other]),
        (hid, hid2.at[me.core], hid2.at[me.other]),
    ]
    swap_in = [rcopy(s, i, pss.at[n], prs.at[n], me.partner) for n, (s, d, i) in enumerate(swap)]
    swap = [rcopy(s, d, pss.at[n], prs.at[n], me.partner) for n, (s, d, i) in enumerate(swap)]
    for r in swap:
        r.start()

    def swap_out(n, src, dst, into):
        r = rcopy(src, dst, pss.at[n], prs.at[n], me.partner)
        swap.append(r)
        r.start()
        return rcopy(src, into, pss.at[n], prs.at[n], me.partner)

    ra, rb = pl.ds(0, 2 * HA), pl.ds(2 * HA, 2 * HB)
    a0, a1, b0, b1 = pl.ds(0, HA), pl.ds(HA, HA), pl.ds(2 * HA, HB), pl.ds(2 * HA + HB, HB)
    ga1 = Gather4(*[lambda j, r=r: wh.at[me.zl, j, r] for r in (ra, a0, a1)], me.x, me.xp, me.xm, wss.at[0], wrs.at[0])
    gb1 = Gather4(*[lambda j, r=r: wh.at[j, me.x, r] for r in (rb, b0, b1)], me.zl, me.zp, me.zm, wss.at[1], wrs.at[1])
    ga2 = Gather4(*[lambda j, r=r: wh.at[j, :, r] for r in (ra, a0, a1)], me.zl, me.zp, me.zm, wss.at[2], wrs.at[2])
    gb2 = Gather4(*[lambda j, r=r: wh.at[:, j, r] for r in (rb, b0, b1)], me.x, me.xp, me.xm, wss.at[3], wrs.at[3])
    all_w = slice(None)
    sa1 = Scatter4(dw, *[lambda j, r=r: (j, all_w, r) for r in (ra, a0, a1)], me.zl, me.zp, me.zm,
                   ha1, wa1, wss.at[4], wrs.at[4])
    sb1 = Scatter4(dw, *[lambda j, r=r: (all_w, j, r) for r in (rb, b0, b1)], me.x, me.xp, me.xm,
                   hb1, wb1, wss.at[5], wrs.at[5])
    sa2 = Scatter4(dw, *[lambda j, r=r: (me.zl, j, r) for r in (ra, a0, a1)], me.x, me.xp, me.xm,
                   ha2, wa2, wss.at[6], wrs.at[6])
    sb2 = Scatter4(dw, *[lambda j, r=r: (j, me.x, r) for r in (rb, b0, b1)], me.zl, me.zp, me.zm,
                   hb2, wb2, wss.at[7], wrs.at[7])

    def spread(buf, n):
        return [(d, rcopy(buf.at[4], buf.at[4 - d], kss.at[n, m], krs.at[n, 4 - d], me.chip(lax.rem(c + d, 8)))) for m, d in enumerate((1, 2, 4))]

    def start_spread(sends):
        for d, r in sends:
            @pl.when(c + d < 8)
            def _():
                r.start()

    passes = (c >= 1) & (c <= 5)

    def forwarding(buf, n):
        return rcopy(buf.at[3], buf.at[1], kss.at[n, 3], krs.at[n, 1], me.chip(lax.rem(c + 2, 8)))

    def arrive(buf, n, j):
        @pl.when(c >= 4 - j)
        def _():
            rcopy(buf.at[4], buf.at[j], kss.at[n, 0], krs.at[n, j], me.chip(lax.rem(c + 4 + j, 8))).wait_recv()

    def forward(buf, n):
        arrive(buf, n, 3)
        @pl.when(passes)
        def _():
            forwarding(buf, n).start()

    def end_spread(buf, n):
        for j in (2, 0, 1):
            arrive(buf, n, j)

    def collecting(buf, into, n, ss, rs):
        to = {0: 4, 1: 2, 2: 2, 3: 1}
        return [rcopy(buf.at[n, j], into.at[n, j], ss.at[n, j], rs.at[n, j], me.chip(lax.rem(c + 8 - to[j], 8))) for j in range(4)]

    def collect(buf, into, n, ss, rs):
        sends = collecting(buf, into, n, ss, rs)
        for j in (1, 0, 2):
            @pl.when(c >= 4 - j)
            def _():
                sends[j].start()
        return sends

    def collect_relay(buf, into, n, ss, rs):
        r = collecting(buf, into, n, ss, rs)
        @pl.when(passes)
        def _():
            r[1].wait_recv()
            buf[n, 3] = (buf[n, 3].astype(F32) + into[n, 1].astype(F32)).astype(BF)
        @pl.when(c >= 1)
        def _():
            r[3].start()

    def collected(buf, into, n, ss, rs):
        acc[...] = buf[n, 4].astype(F32)
        r = collecting(buf, into, n, ss, rs)
        for j, d in ((2, 2), (0, 4), (3, 1)):
            @pl.when(c + d < 8)
            def _():
                r[j].wait_recv()
                acc[...] += into[n, j].astype(F32)
        return acc[...].astype(BF)

    for j in range(4):
        @pl.when(c < 4 - j)
        def _():
            kw[j] = jnp.zeros(kw.shape[1:], BF)
            vw[j] = jnp.zeros(vw.shape[1:], BF)
            dwin[j] = jnp.full(dwin.shape[1:], -1, jnp.int32)

    kd, dd, vd = spread(kw, 0), spread(dwin, 1), spread(vw, 2)
    for n in range(2):
        local[n].wait()
        swap_in[n].wait_recv()
    start_spread(kd)
    start_spread(dd)
    local[2].wait()
    ga1.start()
    gb1.start()
    ga1.relay()
    gb1.relay()
    ga1.finish()
    ga2.start()
    gb1.finish()
    gb2.start()
    forward(kw, 0)
    forward(dwin, 1)
    for n in range(3, 6):
        local[n].wait()
    for n in range(2, 5):
        swap_in[n].wait_recv()
    for z in range(4):
        hidt[z * 1280:(z + 1) * 1280, :] = jnp.transpose(hid2[:, :, z * 1280:(z + 1) * 1280].reshape(256, 1280))
    end_spread(kw, 0)
    end_spread(dwin, 1)
    ga2.relay()
    gb2.relay()
    for t in range(2):
        mine = jnp.transpose(jnp.broadcast_to(dwin[4, t].astype(F32), (BLK, BLK)))
        causal = lax.broadcasted_iota(jnp.int32, (BLK, BLK), 1) <= lax.broadcasted_iota(jnp.int32, (BLK, BLK), 0)
        for b in range(9):
            row = dwin[(b + t) // 2, (b + t) % 2].astype(F32)
            allow = mine == row
            if b == 8:
                allow = allow & causal
            bias[t, :, b * BLK:(b + 1) * BLK] = jnp.where(allow, 0.0, -1e30)

    def window(ref, g, t):
        return ref[:, :, :, g * HS:(g + 1) * HS].reshape(1280, HS)[t * BLK:t * BLK + WIN]

    def first(g, t):
        kk = window(kw, g, t)
        for h in range(G):
            n = (g * 2 + t) * G + h
            col = slice((g * G + h) * HS, (g * G + h + 1) * HS)
            hr = slice(h * BLK, (h + 1) * BLK)
            qq = q2[t, :, col]
            s = dott(qq, kk, 1, 1) + bias[t]
            m = jnp.max(s, axis=1, keepdims=True)
            e = jnp.exp2((s - m) * CC)
            iv = 1.0 / jnp.sum(e, axis=1, keepdims=True)
            eb[g * 2 + t, hr, :] = e.astype(BF)
            inv[n] = iv
            dob[g * 2 + t, hr, :] = (cot2[t, :, col].astype(F32) * iv).astype(BF)
            qs[g * 2 + t, hr, :] = qq
        return dott(eb[g * 2 + t], dob[g * 2 + t], 0, 0)

    def put(buf, g, t, part, scale):
        rows = slice(t * BLK, t * BLK + WIN)
        if t == 0:
            dl[rows, :] = part
            dl[WIN:, :] = jnp.zeros((1280 - WIN, HS), F32)
        else:
            dl[rows, :] += part
            buf[g] = (dl[...] * scale).astype(BF).reshape(5, 256, HS)

    def second(g, t):
        kk, vv = window(kw, g, t), window(vw, g, t)
        for h in range(G):
            n = (g * 2 + t) * G + h
            col = slice((g * G + h) * HS, (g * G + h + 1) * HS)
            hr = slice(h * BLK, (h + 1) * BLK)
            iv = inv[n]
            e = eb[g * 2 + t, hr, :]
            ob = (dott(e, vv, 1, 0) * iv).astype(BF)
            o2[t, :, col] = ob
            delta = jnp.sum(cot2[t, :, col].astype(F32) * ob.astype(F32), axis=1, keepdims=True) * iv
            dp = dott(dob[g * 2 + t, hr, :], vv, 1, 1)
            d = (e.astype(F32) * (dp - delta)).astype(BF)
            ds[hr, :] = d
            dq2[t, :, col] = (dott(d, kk, 1, 0) * SCALE).astype(BF)
        return dott(ds[...], qs[g * 2 + t], 0, 0)

    put(dvb, 0, 0, first(0, 0), 1.0)
    put(dvb, 0, 1, first(0, 1), 1.0)
    sends = collect(dvb, rv, 0, gss, grs)
    put(dvb, 1, 0, first(1, 0), 1.0)
    put(dvb, 1, 1, first(1, 1), 1.0)
    sends += collect(dvb, rv, 1, gss, grs)
    collect_relay(dvb, rv, 0, gss, grs)
    ga2.finish()
    gb2.finish()
    for z in range(4):
        h = hid2[:, :, z * 1280:(z + 1) * 1280].reshape(256, 1280)
        part = jnp.dot(h, wh[z].reshape(1280, 256), preferred_element_type=F32)
        vacc[...] = part if z == 0 else vacc[...] + part
    vw[4] = vacc[...].astype(BF).reshape(2, 128, 256)
    start_spread(vd)
    collect_relay(dvb, rv, 1, gss, grs)

    for g in range(2):
        gvs[:, :, g * HS:(g + 1) * HS] = collected(dvb, rv, g, gss, grs).reshape(2, 128, HS)
    gv = gvs[...].reshape(256, 256)
    for z in range(4):
        dw[z] = jnp.dot(hidt[z * 1280:(z + 1) * 1280, :], gv, preferred_element_type=F32).astype(BF).reshape(4, 320, 256)
    sa1.start()
    sb1.start()
    forward(vw, 2)
    for z in range(4):
        ghp[:, z * 1280:(z + 1) * 1280] = dott(gvs[me.other], wh[z].reshape(1280, 256), 1, 1).astype(BF)
    gh_in = swap_out(5, ghp, ghr, ghr)
    end_spread(vw, 2)
    put(dkb, 0, 0, second(0, 0), SCALE)
    sa1.relay()
    sb1.relay()
    put(dkb, 0, 1, second(0, 1), SCALE)
    sends += collect(dkb, rk, 0, rss, rrs)
    sa1.finish()
    sa2.start()
    sb1.finish()
    sb2.start()
    put(dkb, 1, 0, second(1, 0), SCALE)
    collect_relay(dkb, rk, 0, rss, rrs)
    sa2.relay()
    sb2.relay()
    put(dkb, 1, 1, second(1, 1), SCALE)
    sends += collect(dkb, rk, 1, rss, rrs)
    o_in = swap_out(6, o2.at[me.other], attn.at[:, qcol(me.core)], attn.at[:, qcol(me.other)])
    dq_in = swap_out(7, dq2.at[me.other], gq.at[:, qcol(me.core)], gq.at[:, qcol(me.other)])
    tail = [(o2.at[me.core], attn.at[:, qcol(me.core)]), (dq2.at[me.core], gq.at[:, qcol(me.core)])]
    tail = [pltpu.make_async_copy(s, d, lsem.at[n]) for n, (s, d) in enumerate(tail)]
    for r in tail:
        r.start()
    sa2.finish()
    sb2.finish()

    piece = lambda j: dw.at[me.zl, me.x, pl.ds(mo(j * 80, 16), 80)]
    ychip = lambda d: me.chip(lax.rem(me.y + d, 4) * 2 + me.zh)
    ysend = [rcopy(piece(lax.rem(me.y + d, 4)), yr.at[d - 1], yss.at[d - 1], yrs.at[d - 1], ychip(d)) for d in range(1, 4)]
    for r in ysend:
        r.start()
    for z in range(4):
        cols = slice(z * 1280, (z + 1) * 1280)
        gho[:, cols] = dott(gvs[me.core], wh[z].reshape(1280, 256), 1, 1)
    collect_relay(dkb, rk, 1, rss, rrs)
    tot = dw[me.zl, me.x, pl.ds(mo(me.y * 80, 16), 80)].astype(F32)
    for d in range(3):
        ysend[d].wait_recv()
        tot = tot + yr[d].astype(F32)
    zs[...] = tot.astype(BF)
    zx = rcopy(zs, zr, yss.at[3], yrs.at[3], me.chip(me.y * 2 + 1 - me.zh))
    zx.start()
    gh_in.wait_recv()
    gh[...] = (gho[...] + ghr[...].astype(F32)).astype(BF)
    for g in range(2):
        gkb[:, :, g * HS:(g + 1) * HS] = collected(dkb, rk, g, rss, rrs).reshape(2, 128, HS)
    gk_in = swap_out(8, gkb.at[me.other], gk.at[:, kcol(me.core)], gk.at[:, kcol(me.other)])
    last = pltpu.make_async_copy(gkb.at[me.core], gk.at[:, kcol(me.core)], lsem.at[2])
    last.start()
    zx.wait_recv()
    fin[me.y] = (zs[...].astype(F32) + zr[...].astype(F32)).astype(BF)
    ysend2 = [rcopy(fin.at[me.y], fin.at[me.y], yss.at[3 + d], yrs.at[3 + d], ychip(d)) for d in range(1, 4)]
    for r in ysend2:
        r.start()
    w_in = [swap_out(9, fin.at[me.y], pr.at[me.y], pr.at[me.y])]
    for d in range(1, 4):
        j = lax.rem(me.y + 4 - d, 4)
        rcopy(fin.at[j], fin.at[j], yss.at[3 + d], yrs.at[3 + d], ychip(d)).wait_recv()
        w_in.append(swap_out(9 + d, fin.at[j], pr.at[j], pr.at[j]))
    gw[:, kcol(me.core)] = fin[...].astype(F32).reshape(320, 256)
    for r in w_in:
        r.wait_recv()
    gw[:, kcol(me.other)] = pr[...].astype(F32).reshape(320, 256)
    for r in tail + [last]:
        r.wait()
    for r in (o_in, dq_in, gk_in):
        r.wait_recv()
    for r in swap + ysend + ysend2 + [zx]:
        r.wait_send()
    for n, (buf, p) in enumerate(((kw, kd), (dwin, dd), (vw, vd))):
        for d, r in p:
            @pl.when(c + d < 8)
            def _():
                r.wait_send()
        @pl.when(passes)
        def _():
            forwarding(buf, n).wait_send()
    for n, r in enumerate(sends):
        @pl.when(c >= 4 - n % 4)
        def _():
            r.wait_send()
    for g in (ga1, gb1, ga2, gb2, sa1, sb1, sa2, sb2):
        g.drain()


def mega(w, hid, q, cot, k, docs):
    shp = jax.ShapeDtypeStruct
    vm = pl.BlockSpec(memory_space=pltpu.VMEM)
    dma = pltpu.SemaphoreType.DMA
    v = pltpu.VMEM
    return pl.pallas_call(
        mega_kernel,
        out_shape=(
            shp((128, 2560), BF), shp((128, 2560), BF), shp((128, 512), BF), shp((128, 5120), BF), shp((320, 512), F32),
        ),
        in_specs=[pl.BlockSpec(memory_space=pltpu.HBM)] * 6,
        out_specs=(vm,) * 5,
        scratch_shapes=[
            v((4, 4, 320, 256), BF), v((2, 128, 5120), BF), v((5120, 256), BF), v((2, 128, 1280), BF), v((2, 128, 1280), BF),
            v((5, 2, 128, 256), BF), v((5, 2, 128, 256), BF), v((5, 2, 1, 128), jnp.int32), v((256, 256), F32),
            v((2, BLK, WIN), F32), v((4, G * BLK, WIN), BF), v((G * BLK, WIN), BF), v((4, G * BLK, HS), BF), v((4, G * BLK, HS), BF),
            v((20, BLK, 1), F32), v((1280, HS), F32), v((256, HS), F32),
            v((2, 5, 256, HS), BF), v((2, 4, 256, HS), BF), v((2, 5, 256, HS), BF), v((2, 4, 256, HS), BF),
            v((2, 128, 1280), BF), v((2, 128, 1280), BF), v((2, 128, 256), BF), v((2, 128, 256), BF),
            v((128, 5120), BF), v((128, 5120), BF), v((128, 5120), F32), v((4, 4, 320, 256), BF),
            v((2, 4, HA, 256), BF), v((2, 4, 2 * HA, 256), BF), v((2, 4, HB, 256), BF), v((2, 4, 2 * HB, 256), BF),
            v((2, HA, 256), BF), v((2, 2 * HA, 256), BF), v((2, HB, 256), BF), v((2, 2 * HB, 256), BF),
            v((3, 80, 256), BF), v((80, 256), BF), v((80, 256), BF), v((4, 80, 256), BF), v((4, 80, 256), BF),
            dma((8, 4)), dma((8, 4)), dma((13,)), dma((13,)), dma((6,)), dma((3, 4)), dma((3, 4)),
            dma((2, 4)), dma((2, 4)), dma((2, 4)), dma((2, 4)), dma((7,)), dma((7,)),
        ],
        compiler_params=pltpu.CompilerParams(collective_id=0, has_side_effects=True, vmem_limit_bytes=44 << 20),
        name="whole",
    )(w, hid, q, cot, k, docs)


def flush_kernel(*refs):
    sem = refs[10]
    copies = [pltpu.make_async_copy(refs[n], refs[5 + n], sem.at[n]) for n in range(5)]
    for r in copies:
        r.start()
    for r in copies:
        r.wait()


def flush(*arrays):
    return pl.pallas_call(
        flush_kernel,
        out_shape=tuple(jax.ShapeDtypeStruct(a.shape, a.dtype) for a in arrays),
        in_specs=[pl.BlockSpec(memory_space=pltpu.VMEM)] * 5,
        out_specs=(pl.BlockSpec(memory_space=pl.ANY),) * 5,
        scratch_shapes=[pltpu.SemaphoreType.DMA((5,))],
        compiler_params=pltpu.CompilerParams(vmem_limit_bytes=4 << 20),
        name="flush",
    )(*arrays)


def body(hidden, queries, keys, value_weight, doc_ids, cotangent):
    attn, gq, gk, gh, gw = flush(*mega(*[pltpu.with_memory_space_constraint(a, pltpu.HBM) for a in (value_weight, hidden[0], queries[0], cotangent[0], keys[0], doc_ids)]))
    return attn[None], gq[None], gk[None], gh[None], gw


def solution(mesh):
    rows = P("dp", "seq", None)
    return jax.shard_map(
        body, mesh=mesh,
        in_specs=(rows, rows, rows, P("dp", None), P("dp", "seq"), rows),
        out_specs=(rows, rows, rows, rows, P("dp", None)),
        check_vma=False,
    )
```

```python
import jax
import jax.numpy as jnp
from jax import lax
from jax.experimental import pallas as pl
from jax.experimental.pallas import tpu as pltpu
from jax.sharding import PartitionSpec as P

HS = 128
G = 5
BLK = 128
WIN = 9 * BLK
CC = HS ** -0.5 * 1.4426950408889634
SCALE = HS ** -0.5

def dott(a, b, ca, cb):
    return lax.dot_general(a, b, (((ca,), (cb,)), ((), ())), preferred_element_type=jnp.float32)

MESH = pl.DeviceIdType.MESH
BF = jnp.bfloat16
F32 = jnp.float32


def rcopy(src, dst, ssem, rsem, dev):
    return pltpu.make_async_remote_copy(
        src_ref=src, dst_ref=dst, send_sem=ssem, recv_sem=rsem, device_id=dev, device_id_type=MESH
    )


def mo(v, n):
    return pl.multiple_of(v, n)


class Where:
    def __init__(self):
        a, s = lax.axis_index("dp"), lax.axis_index("seq")
        self.a, self.s = a, s
        self.zl, self.x = a // 4, lax.rem(a, 4)
        self.core, self.c = lax.rem(s, 2), s // 2
        self.y, self.zh = self.c // 2, lax.rem(self.c, 2)
        self.other = 1 - self.core
        self.partner = (a, self.c * 2 + self.other)
        self.xp, self.xm = self.at_x(1), self.at_x(3)
        self.zp, self.zm = self.at_z(1), self.at_z(7)

    def at_x(self, d):
        return (self.zl * 4 + lax.rem(self.x + d, 4), self.s)

    def at_z(self, d):
        z = lax.rem(self.zh * 4 + self.zl + d, 8)
        return (lax.rem(z, 4) * 4 + self.x, (self.y * 2 + z // 4) * 2 + self.core)

    def chip(self, c):
        return (self.a, c * 2 + self.core)

    def enter(self):
        barrier = pltpu.get_barrier_semaphore()
        peers = [self.partner, self.xp, self.xm, self.zp, self.zm]
        peers += [self.chip(lax.rem(self.c + d, 8)) for d in range(1, 8)]
        for p in peers:
            pl.semaphore_signal(barrier, inc=1, device_id=p, device_id_type=MESH)
        pl.semaphore_wait(barrier, len(peers))


class Gather4:
    def __init__(self, blk, h0, h1, i, p, m, ss, rs):
        one, two, three = lax.rem(i + 1, 4), lax.rem(i + 2, 4), lax.rem(i + 3, 4)
        self.first = [rcopy(blk(i), blk(i), ss.at[0], rs.at[0], p), rcopy(blk(i), blk(i), ss.at[1], rs.at[1], m)]
        self.first_in = [rcopy(blk(three), blk(three), ss.at[0], rs.at[0], p), rcopy(blk(one), blk(one), ss.at[1], rs.at[1], m)]
        self.second = [rcopy(h0(three), h0(three), ss.at[2], rs.at[2], p), rcopy(h1(one), h1(one), ss.at[3], rs.at[3], m)]
        self.second_in = [rcopy(h0(two), h0(two), ss.at[2], rs.at[2], p), rcopy(h1(two), h1(two), ss.at[3], rs.at[3], m)]

    def start(self):
        for r in self.first:
            r.start()

    def relay(self):
        for got, go in zip(self.first_in, self.second):
            got.wait_recv()
            go.start()

    def finish(self):
        for r in self.second_in:
            r.wait_recv()

    def drain(self):
        for r in self.first + self.second:
            r.wait_send()


class Scatter4:
    def __init__(self, ref, at, h0, h1, i, p, m, halves, wholes, ss, rs):
        self.ref, self.at, self.h0, self.h1, self.i = ref, at, h0, h1, i
        self.halves, self.wholes = halves, wholes
        one, two, three = lax.rem(i + 1, 4), lax.rem(i + 2, 4), lax.rem(i + 3, 4)
        self.one, self.three = one, three
        self.first = [
            rcopy(ref.at[h0(two)], halves.at[0], ss.at[0], rs.at[0], p),
            rcopy(ref.at[h1(two)], halves.at[1], ss.at[1], rs.at[1], m),
        ]
        self.second = [
            rcopy(ref.at[at(one)], wholes.at[0], ss.at[2], rs.at[2], p),
            rcopy(ref.at[at(three)], wholes.at[1], ss.at[3], rs.at[3], m),
        ]

    def start(self):
        for r in self.first:
            r.start()

    def relay(self):
        for n, where in ((0, self.h0(self.one)), (1, self.h1(self.three))):
            self.first[n].wait_recv()
            self.ref[where] = (self.ref[where].astype(F32) + self.halves[n].astype(F32)).astype(BF)
            self.second[n].start()

    def finish(self):
        for r in self.second:
            r.wait_recv()
        own = self.at(self.i)
        self.ref[own] = (
            self.ref[own].astype(F32) + self.wholes[0].astype(F32) + self.wholes[1].astype(F32)
        ).astype(BF)

    def drain(self):
        for r in self.first + self.second:
            r.wait_send()


HA, HB = 80, 80


def mega_kernel(w, hid, q, cot, k, docs, attn, gq, gk, gh, gw,
                wh, hid2, hidt, q2, cot2, kw, vw, dwin, vacc, bias, eb, ds, dob, qs, inv, dl, acc,
                dvb, rv, dkb, rk, o2, dq2, gkb, gvs, ghp, ghr, gho, dw, ha1, wa1, hb1, wb1, ha2, wa2, hb2, wb2,
                yr, zs, zr, fin, pr, wss, wrs, pss, prs, lsem, kss, krs, gss, grs, rss, rrs, yss, yrs):
    me = Where()
    c = me.c
    qcol = lambda n: pl.ds(mo(n * 1280, 128), 1280)
    kcol = lambda n: pl.ds(mo(n * 256, 128), 256)
    hcol = lambda n, g: pl.ds(mo(n * 256 + g * HS, 128), HS)
    local = [
        (k.at[:, hcol(me.core, 0)], kw.at[0, 4, me.core]),
        (docs, dwin.at[4, me.core]),
        (k.at[:, hcol(me.core, 1)], kw.at[1, 4, me.core]),
        (w.at[:, kcol(me.core)], wh.at[me.zl, me.x]),
        (hid, hid2.at[me.core]),
        (q.at[:, qcol(me.core)], q2.at[me.core]),
        (cot.at[:, qcol(me.core)], cot2.at[me.core]),
    ]
    local = [pltpu.make_async_copy(s, d, lsem.at[n]) for n, (s, d) in enumerate(local)]
    for r in local:
        r.start()
    me.enter()
    swap = [
        (k.at[:, hcol(me.other, 0)], kw.at[0, 4, me.core], kw.at[0, 4, me.other]),
        (docs, dwin.at[4, me.core], dwin.at[4, me.other]),
        (k.at[:, hcol(me.other, 1)], kw.at[1, 4, me.core], kw.at[1, 4, me.other]),
        (q.at[:, qcol(me.other)], q2.at[me.core], q2.at[me.other]),
        (cot.at[:, qcol(me.other)], cot2.at[me.core], cot2.at[me.other]),
        (hid, hid2.at[me.core], hid2.at[me.other]),
    ]
    swap_in = [rcopy(s, i, pss.at[n], prs.at[n], me.partner) for n, (s, d, i) in enumerate(swap)]
    swap = [rcopy(s, d, pss.at[n], prs.at[n], me.partner) for n, (s, d, i) in enumerate(swap)]
    for r in swap:
        r.start()

    def swap_out(n, src, dst, into):
        r = rcopy(src, dst, pss.at[n], prs.at[n], me.partner)
        swap.append(r)
        r.start()
        return rcopy(src, into, pss.at[n], prs.at[n], me.partner)

    ra, rb = pl.ds(0, 2 * HA), pl.ds(2 * HA, 2 * HB)
    a0, a1, b0, b1 = pl.ds(0, HA), pl.ds(HA, HA), pl.ds(2 * HA, HB), pl.ds(2 * HA + HB, HB)
    ga1 = Gather4(*[lambda j, r=r: wh.at[me.zl, j, r] for r in (ra, a0, a1)], me.x, me.xp, me.xm, wss.at[0], wrs.at[0])
    gb1 = Gather4(*[lambda j, r=r: wh.at[j, me.x, r] for r in (rb, b0, b1)], me.zl, me.zp, me.zm, wss.at[1], wrs.at[1])
    near = lambda i, n: lax.rem(i + n, 4)
    ga2 = [Gather4(*[lambda j, r=r, n=n: wh.at[j, near(me.x, n), r] for r in (ra, a0, a1)], me.zl, me.zp, me.zm, wss.at[2 + n], wrs.at[2 + n]) for n in range(4)]
    gb2 = [Gather4(*[lambda j, r=r, n=n: wh.at[near(me.zl, n), j, r] for r in (rb, b0, b1)], me.x, me.xp, me.xm, wss.at[6 + n], wrs.at[6 + n]) for n in range(4)]
    sa1 = [Scatter4(dw, *[lambda j, r=r, n=n: (j, near(me.x, n), r) for r in (ra, a0, a1)], me.zl, me.zp, me.zm,
                    ha1.at[n], wa1.at[n], wss.at[10 + n], wrs.at[10 + n]) for n in range(4)]
    sb1 = [Scatter4(dw, *[lambda j, r=r, n=n: (near(me.zl, n), j, r) for r in (rb, b0, b1)], me.x, me.xp, me.xm,
                    hb1.at[n], wb1.at[n], wss.at[14 + n], wrs.at[14 + n]) for n in range(4)]
    sa2 = Scatter4(dw, *[lambda j, r=r: (me.zl, j, r) for r in (ra, a0, a1)], me.x, me.xp, me.xm,
                   ha2, wa2, wss.at[18], wrs.at[18])
    sb2 = Scatter4(dw, *[lambda j, r=r: (j, me.x, r) for r in (rb, b0, b1)], me.zl, me.zp, me.zm,
                   hb2, wb2, wss.at[19], wrs.at[19])

    def spread(buf, n):
        return [(d, rcopy(buf.at[4], buf.at[4 - d], kss.at[n, m], krs.at[n, 4 - d], me.chip(lax.rem(c + d, 8)))) for m, d in enumerate((1, 2, 4))]

    def start_spread(sends):
        for d, r in sends:
            @pl.when(c + d < 8)
            def _():
                r.start()

    passes = (c >= 1) & (c <= 5)

    def forwarding(buf, n):
        return rcopy(buf.at[3], buf.at[1], kss.at[n, 3], krs.at[n, 1], me.chip(lax.rem(c + 2, 8)))

    def arrive(buf, n, j):
        @pl.when(c >= 4 - j)
        def _():
            rcopy(buf.at[4], buf.at[j], kss.at[n, 0], krs.at[n, j], me.chip(lax.rem(c + 4 + j, 8))).wait_recv()

    def forward(buf, n):
        arrive(buf, n, 3)
        @pl.when(passes)
        def _():
            forwarding(buf, n).start()

    def end_spread(buf, n):
        for j in (2, 0, 1):
            arrive(buf, n, j)

    def collecting(buf, into, n, ss, rs):
        to = {0: 4, 1: 2, 2: 2, 3: 1}
        return [rcopy(buf.at[n, j], into.at[n, j], ss.at[n, j], rs.at[n, j], me.chip(lax.rem(c + 8 - to[j], 8))) for j in range(4)]

    def collect(buf, into, n, ss, rs):
        sends = collecting(buf, into, n, ss, rs)
        for j in (1, 0, 2):
            @pl.when(c >= 4 - j)
            def _():
                sends[j].start()
        return sends

    def collect_relay(buf, into, n, ss, rs):
        r = collecting(buf, into, n, ss, rs)
        @pl.when(passes)
        def _():
            r[1].wait_recv()
            buf[n, 3] = (buf[n, 3].astype(F32) + into[n, 1].astype(F32)).astype(BF)
        @pl.when(c >= 1)
        def _():
            r[3].start()

    def collected(buf, into, n, ss, rs):
        acc[...] = buf[n, 4].astype(F32)
        r = collecting(buf, into, n, ss, rs)
        for j, d in ((2, 2), (0, 4), (3, 1)):
            @pl.when(c + d < 8)
            def _():
                r[j].wait_recv()
                acc[...] += into[n, j].astype(F32)
        return acc[...].astype(BF)

    for j in range(4):
        @pl.when(c < 4 - j)
        def _():
            for g in range(2):
                kw[g, j] = jnp.zeros(kw.shape[2:], BF)
                vw[g, j] = jnp.zeros(vw.shape[2:], BF)
            dwin[j] = jnp.full(dwin.shape[1:], -1, jnp.int32)

    flows = [(kw.at[0], 0), (dwin, 1), (kw.at[1], 2), (vw.at[0], 3), (vw.at[1], 4)]
    going = [spread(*f) for f in flows]
    for n in range(3):
        local[n].wait()
        swap_in[n].wait_recv()
        start_spread(going[n])
    local[3].wait()
    ga1.start()
    gb1.start()
    ga2[0].start()
    gb2[0].start()
    for g1, g2 in ((ga1, ga2), (gb1, gb2)):
        g1.relay()
        g2[3].start()
        g2[1].start()
    for g1, g2 in ((ga1, ga2), (gb1, gb2)):
        g1.finish()
        g2[2].start()
    ga2[0].relay()
    gb2[0].relay()
    for f in flows[:3]:
        forward(*f)
    for n in range(4, 7):
        local[n].wait()
    for n in range(3, 6):
        swap_in[n].wait_recv()

    def turn(z):
        hidt[z * 1280:(z + 1) * 1280, :] = jnp.transpose(hid2[:, :, z * 1280:(z + 1) * 1280].reshape(256, 1280))

    turn(0)
    turn(1)
    for n in (3, 1):
        ga2[n].relay()
        gb2[n].relay()
    turn(2)
    turn(3)
    end_spread(*flows[0])
    end_spread(*flows[1])
    ga2[2].relay()
    gb2[2].relay()
    for t in range(2):
        mine = jnp.transpose(jnp.broadcast_to(dwin[4, t].astype(F32), (BLK, BLK)))
        causal = lax.broadcasted_iota(jnp.int32, (BLK, BLK), 1) <= lax.broadcasted_iota(jnp.int32, (BLK, BLK), 0)
        for b in range(9):
            row = dwin[(b + t) // 2, (b + t) % 2].astype(F32)
            allow = mine == row
            if b == 8:
                allow = allow & causal
            bias[t, :, b * BLK:(b + 1) * BLK] = jnp.where(allow, 0.0, -1e30)

    def window(ref, g, t):
        return ref[g].reshape(1280, HS)[t * BLK:t * BLK + WIN]

    def first(g, t):
        kk = window(kw, g, t)
        for h in range(G):
            n = (g * 2 + t) * G + h
            col = slice((g * G + h) * HS, (g * G + h + 1) * HS)
            hr = slice(h * BLK, (h + 1) * BLK)
            qq = q2[t, :, col]
            s = dott(qq, kk, 1, 1) + bias[t]
            m = jnp.max(s, axis=1, keepdims=True)
            e = jnp.exp2((s - m) * CC)
            iv = 1.0 / jnp.sum(e, axis=1, keepdims=True)
            eb[g * 2 + t, hr, :] = e.astype(BF)
            inv[n] = iv
            dob[g * 2 + t, hr, :] = (cot2[t, :, col].astype(F32) * iv).astype(BF)
            qs[g * 2 + t, hr, :] = qq
        return dott(eb[g * 2 + t], dob[g * 2 + t], 0, 0)

    def put(buf, g, t, part, scale):
        rows = slice(t * BLK, t * BLK + WIN)
        if t == 0:
            dl[rows, :] = part
            dl[WIN:, :] = jnp.zeros((1280 - WIN, HS), F32)
        else:
            dl[rows, :] += part
            buf[g] = (dl[...] * scale).astype(BF).reshape(5, 256, HS)

    def second(g, t):
        kk, vv = window(kw, g, t), window(vw, g, t)
        for h in range(G):
            n = (g * 2 + t) * G + h
            col = slice((g * G + h) * HS, (g * G + h + 1) * HS)
            hr = slice(h * BLK, (h + 1) * BLK)
            iv = inv[n]
            e = eb[g * 2 + t, hr, :]
            ob = (dott(e, vv, 1, 0) * iv).astype(BF)
            o2[t, :, col] = ob
            delta = jnp.sum(cot2[t, :, col].astype(F32) * ob.astype(F32), axis=1, keepdims=True) * iv
            dp = dott(dob[g * 2 + t, hr, :], vv, 1, 1)
            d = (e.astype(F32) * (dp - delta)).astype(BF)
            ds[hr, :] = d
            dq2[t, :, col] = (dott(d, kk, 1, 0) * SCALE).astype(BF)
        return dott(ds[...], qs[g * 2 + t], 0, 0)

    put(dvb, 0, 0, first(0, 0), 1.0)
    put(dvb, 0, 1, first(0, 1), 1.0)
    sends = collect(dvb, rv, 0, gss, grs)
    end_spread(*flows[2])
    put(dvb, 1, 0, first(1, 0), 1.0)
    put(dvb, 1, 1, first(1, 1), 1.0)
    sends += collect(dvb, rv, 1, gss, grs)
    collect_relay(dvb, rv, 0, gss, grs)
    for n in range(4):
        ga2[n].finish()
        gb2[n].finish()
    for z in range(4):
        h = hid2[:, :, z * 1280:(z + 1) * 1280].reshape(256, 1280)
        part = jnp.dot(h, wh[z].reshape(1280, 256), preferred_element_type=F32)
        vacc[...] = part if z == 0 else vacc[...] + part
    for g in range(2):
        vw[g, 4] = vacc[:, g * HS:(g + 1) * HS].astype(BF).reshape(2, 128, HS)
    start_spread(going[3])
    start_spread(going[4])
    collect_relay(dvb, rv, 1, gss, grs)
    for g in range(2):
        gvs[:, :, g * HS:(g + 1) * HS] = collected(dvb, rv, g, gss, grs).reshape(2, 128, HS)
    gv = gvs[...].reshape(256, 256)
    for z in range(4):
        dw[z] = jnp.dot(hidt[z * 1280:(z + 1) * 1280, :], gv, preferred_element_type=F32).astype(BF).reshape(4, 320, 256)
    order = (2, 1, 3, 0)
    for n in order:
        sa1[n].start()
        sb1[n].start()
    forward(*flows[3])
    forward(*flows[4])
    for z in range(4):
        ghp[:, z * 1280:(z + 1) * 1280] = dott(gvs[me.other], wh[z].reshape(1280, 256), 1, 1).astype(BF)
    gh_in = swap_out(6, ghp, ghr, ghr)
    for n in order:
        sa1[n].relay()
        sb1[n].relay()
    end_spread(*flows[3])
    put(dkb, 0, 0, second(0, 0), SCALE)
    sa1[2].finish()
    sa2.start()
    sb1[2].finish()
    sb2.start()
    put(dkb, 0, 1, second(0, 1), SCALE)
    sends += collect(dkb, rk, 0, rss, rrs)
    for n in (1, 3):
        sa1[n].finish()
        sb1[n].finish()
    sa2.relay()
    sb2.relay()
    end_spread(*flows[4])
    put(dkb, 1, 0, second(1, 0), SCALE)
    sa1[0].finish()
    sb1[0].finish()
    sa2.finish()
    sb2.finish()
    piece = lambda j: dw.at[me.zl, me.x, pl.ds(mo(j * 80, 16), 80)]
    ychip = lambda d: me.chip(lax.rem(me.y + d, 4) * 2 + me.zh)
    ysend = [rcopy(piece(lax.rem(me.y + d, 4)), yr.at[d - 1], yss.at[d - 1], yrs.at[d - 1], ychip(d)) for d in range(1, 4)]
    for r in ysend:
        r.start()
    collect_relay(dkb, rk, 0, rss, rrs)
    put(dkb, 1, 1, second(1, 1), SCALE)
    sends += collect(dkb, rk, 1, rss, rrs)
    tot = dw[me.zl, me.x, pl.ds(mo(me.y * 80, 16), 80)].astype(F32)
    for d in range(3):
        ysend[d].wait_recv()
        tot = tot + yr[d].astype(F32)
    zs[...] = tot.astype(BF)
    zx = rcopy(zs, zr, yss.at[3], yrs.at[3], me.chip(me.y * 2 + 1 - me.zh))
    zx.start()
    o_in = swap_out(7, o2.at[me.other], attn.at[:, qcol(me.core)], attn.at[:, qcol(me.other)])
    dq_in = swap_out(8, dq2.at[me.other], gq.at[:, qcol(me.core)], gq.at[:, qcol(me.other)])
    tail = [(o2.at[me.core], attn.at[:, qcol(me.core)]), (dq2.at[me.core], gq.at[:, qcol(me.core)])]
    tail = [pltpu.make_async_copy(s, d, lsem.at[n]) for n, (s, d) in enumerate(tail)]
    for r in tail:
        r.start()
    for z in range(4):
        cols = slice(z * 1280, (z + 1) * 1280)
        gho[:, cols] = dott(gvs[me.core], wh[z].reshape(1280, 256), 1, 1)
    collect_relay(dkb, rk, 1, rss, rrs)
    gh_in.wait_recv()
    gh[...] = (gho[...] + ghr[...].astype(F32)).astype(BF)
    zx.wait_recv()
    fin[me.y] = (zs[...].astype(F32) + zr[...].astype(F32)).astype(BF)
    ysend2 = [rcopy(fin.at[me.y], fin.at[me.y], yss.at[3 + d], yrs.at[3 + d], ychip(d)) for d in range(1, 4)]
    for r in ysend2:
        r.start()
    w_in = [swap_out(10, fin.at[me.y], pr.at[me.y], pr.at[me.y])]
    for g in range(2):
        gkb[:, :, g * HS:(g + 1) * HS] = collected(dkb, rk, g, rss, rrs).reshape(2, 128, HS)
    gk_in = swap_out(9, gkb.at[me.other], gk.at[:, kcol(me.core)], gk.at[:, kcol(me.other)])
    last = pltpu.make_async_copy(gkb.at[me.core], gk.at[:, kcol(me.core)], lsem.at[2])
    last.start()
    for d in range(1, 4):
        j = lax.rem(me.y + 4 - d, 4)
        rcopy(fin.at[j], fin.at[j], yss.at[3 + d], yrs.at[3 + d], ychip(d)).wait_recv()
        w_in.append(swap_out(10 + d, fin.at[j], pr.at[j], pr.at[j]))
    gw[:, kcol(me.core)] = fin[...].astype(F32).reshape(320, 256)
    for r in w_in:
        r.wait_recv()
    gw[:, kcol(me.other)] = pr[...].astype(F32).reshape(320, 256)
    for r in tail + [last]:
        r.wait()
    for r in (o_in, dq_in, gk_in):
        r.wait_recv()
    for r in swap + ysend + ysend2 + [zx]:
        r.wait_send()
    for f, p in zip(flows, going):
        for d, r in p:
            @pl.when(c + d < 8)
            def _():
                r.wait_send()
        @pl.when(passes)
        def _():
            forwarding(*f).wait_send()
    for n, r in enumerate(sends):
        @pl.when(c >= 4 - n % 4)
        def _():
            r.wait_send()
    for g in (ga1, gb1, *ga2, *gb2, *sa1, *sb1, sa2, sb2):
        g.drain()


def mega(w, hid, q, cot, k, docs):
    shp = jax.ShapeDtypeStruct
    vm = pl.BlockSpec(memory_space=pltpu.VMEM)
    dma = pltpu.SemaphoreType.DMA
    v = pltpu.VMEM
    return pl.pallas_call(
        mega_kernel,
        out_shape=(
            shp((128, 2560), BF), shp((128, 2560), BF), shp((128, 512), BF), shp((128, 5120), BF), shp((320, 512), F32),
        ),
        in_specs=[pl.BlockSpec(memory_space=pltpu.HBM)] * 6,
        out_specs=(vm,) * 5,
        scratch_shapes=[
            v((4, 4, 320, 256), BF), v((2, 128, 5120), BF), v((5120, 256), BF), v((2, 128, 1280), BF), v((2, 128, 1280), BF),
            v((2, 5, 2, 128, HS), BF), v((2, 5, 2, 128, HS), BF), v((5, 2, 1, 128), jnp.int32), v((256, 256), F32),
            v((2, BLK, WIN), F32), v((4, G * BLK, WIN), BF), v((G * BLK, WIN), BF), v((4, G * BLK, HS), BF), v((4, G * BLK, HS), BF),
            v((20, BLK, 1), F32), v((1280, HS), F32), v((256, HS), F32),
            v((2, 5, 256, HS), BF), v((2, 4, 256, HS), BF), v((2, 5, 256, HS), BF), v((2, 4, 256, HS), BF),
            v((2, 128, 1280), BF), v((2, 128, 1280), BF), v((2, 128, 256), BF), v((2, 128, 256), BF),
            v((128, 5120), BF), v((128, 5120), BF), v((128, 5120), F32), v((4, 4, 320, 256), BF),
            v((4, 2, HA, 256), BF), v((4, 2, 2 * HA, 256), BF), v((4, 2, HB, 256), BF), v((4, 2, 2 * HB, 256), BF),
            v((2, HA, 256), BF), v((2, 2 * HA, 256), BF), v((2, HB, 256), BF), v((2, 2 * HB, 256), BF),
            v((3, 80, 256), BF), v((80, 256), BF), v((80, 256), BF), v((4, 80, 256), BF), v((4, 80, 256), BF),
            dma((20, 4)), dma((20, 4)), dma((14,)), dma((14,)), dma((7,)), dma((5, 4)), dma((5, 4)),
            dma((2, 4)), dma((2, 4)), dma((2, 4)), dma((2, 4)), dma((7,)), dma((7,)),
        ],
        compiler_params=pltpu.CompilerParams(collective_id=0, has_side_effects=True, vmem_limit_bytes=44 << 20),
        name="whole",
    )(w, hid, q, cot, k, docs)


def flush_kernel(*refs):
    sem = refs[10]
    copies = [pltpu.make_async_copy(refs[n], refs[5 + n], sem.at[n]) for n in range(5)]
    for r in copies:
        r.start()
    for r in copies:
        r.wait()


def flush(*arrays):
    return pl.pallas_call(
        flush_kernel,
        out_shape=tuple(jax.ShapeDtypeStruct(a.shape, a.dtype) for a in arrays),
        in_specs=[pl.BlockSpec(memory_space=pltpu.VMEM)] * 5,
        out_specs=(pl.BlockSpec(memory_space=pl.ANY),) * 5,
        scratch_shapes=[pltpu.SemaphoreType.DMA((5,))],
        compiler_params=pltpu.CompilerParams(vmem_limit_bytes=4 << 20),
        name="flush",
    )(*arrays)


def body(hidden, queries, keys, value_weight, doc_ids, cotangent):
    attn, gq, gk, gh, gw = flush(*mega(*[pltpu.with_memory_space_constraint(a, pltpu.HBM) for a in (value_weight, hidden[0], queries[0], cotangent[0], keys[0], doc_ids)]))
    return attn[None], gq[None], gk[None], gh[None], gw


def solution(mesh):
    rows = P("dp", "seq", None)
    return jax.shard_map(
        body, mesh=mesh,
        in_specs=(rows, rows, rows, P("dp", None), P("dp", "seq"), rows),
        out_specs=(rows, rows, rows, rows, P("dp", None)),
        check_vma=False,
    )
```

```python
import jax
import jax.numpy as jnp
from jax import lax
from jax.experimental import pallas as pl
from jax.experimental.pallas import tpu as pltpu
from jax.sharding import PartitionSpec as P

HS = 128
G = 5
BLK = 128
WIN = 9 * BLK
CC = HS ** -0.5 * 1.4426950408889634
SCALE = HS ** -0.5

def dott(a, b, ca, cb):
    return lax.dot_general(a, b, (((ca,), (cb,)), ((), ())), preferred_element_type=jnp.float32)

MESH = pl.DeviceIdType.MESH
BF = jnp.bfloat16
F32 = jnp.float32


def rcopy(src, dst, ssem, rsem, dev):
    return pltpu.make_async_remote_copy(
        src_ref=src, dst_ref=dst, send_sem=ssem, recv_sem=rsem, device_id=dev, device_id_type=MESH
    )


def mo(v, n):
    return pl.multiple_of(v, n)


class Where:
    def __init__(self):
        a, s = lax.axis_index("dp"), lax.axis_index("seq")
        self.a, self.s = a, s
        self.zl, self.x = a // 4, lax.rem(a, 4)
        self.core, self.c = lax.rem(s, 2), s // 2
        self.y, self.zh = self.c // 2, lax.rem(self.c, 2)
        self.other = 1 - self.core
        self.partner = (a, self.c * 2 + self.other)
        self.xp, self.xm = self.at_x(1), self.at_x(3)
        self.zp, self.zm = self.at_z(1), self.at_z(7)

    def at_x(self, d):
        return (self.zl * 4 + lax.rem(self.x + d, 4), self.s)

    def at_z(self, d):
        z = lax.rem(self.zh * 4 + self.zl + d, 8)
        return (lax.rem(z, 4) * 4 + self.x, (self.y * 2 + z // 4) * 2 + self.core)

    def chip(self, c):
        return (self.a, c * 2 + self.core)

    def enter(self):
        barrier = pltpu.get_barrier_semaphore()
        peers = [self.partner, self.xp, self.xm, self.zp, self.zm]
        peers += [self.chip(lax.rem(self.c + d, 8)) for d in (1, 2, 4, 6, 7)]
        for p in peers:
            pl.semaphore_signal(barrier, inc=1, device_id=p, device_id_type=MESH)
        pl.semaphore_wait(barrier, len(peers))


class Gather4:
    def __init__(self, blk, h0, h1, i, p, m, ss, rs):
        one, two, three = lax.rem(i + 1, 4), lax.rem(i + 2, 4), lax.rem(i + 3, 4)
        self.first = [rcopy(blk(i), blk(i), ss.at[0], rs.at[0], p), rcopy(blk(i), blk(i), ss.at[1], rs.at[1], m)]
        self.first_in = [rcopy(blk(three), blk(three), ss.at[0], rs.at[0], p), rcopy(blk(one), blk(one), ss.at[1], rs.at[1], m)]
        self.second = [rcopy(h0(three), h0(three), ss.at[2], rs.at[2], p), rcopy(h1(one), h1(one), ss.at[3], rs.at[3], m)]
        self.second_in = [rcopy(h0(two), h0(two), ss.at[2], rs.at[2], p), rcopy(h1(two), h1(two), ss.at[3], rs.at[3], m)]

    def start(self):
        for r in self.first:
            r.start()

    def relay(self):
        for got, go in zip(self.first_in, self.second):
            got.wait_recv()
            go.start()

    def finish(self):
        for r in self.second_in:
            r.wait_recv()

    def drain(self):
        for r in self.first + self.second:
            r.wait_send()


class Scatter4:
    def __init__(self, ref, at, h0, h1, i, p, m, halves, wholes, ss, rs):
        self.ref, self.at, self.h0, self.h1, self.i = ref, at, h0, h1, i
        self.halves, self.wholes = halves, wholes
        one, two, three = lax.rem(i + 1, 4), lax.rem(i + 2, 4), lax.rem(i + 3, 4)
        self.one, self.three = one, three
        self.first = [
            rcopy(ref.at[h0(two)], halves.at[0], ss.at[0], rs.at[0], p),
            rcopy(ref.at[h1(two)], halves.at[1], ss.at[1], rs.at[1], m),
        ]
        self.second = [
            rcopy(ref.at[at(one)], wholes.at[0], ss.at[2], rs.at[2], p),
            rcopy(ref.at[at(three)], wholes.at[1], ss.at[3], rs.at[3], m),
        ]

    def start(self):
        for r in self.first:
            r.start()

    def relay(self):
        for n, where in ((0, self.h0(self.one)), (1, self.h1(self.three))):
            self.first[n].wait_recv()
            self.ref[where] = (self.ref[where].astype(F32) + self.halves[n].astype(F32)).astype(BF)
            self.second[n].start()

    def finish(self):
        for r in self.second:
            r.wait_recv()
        own = self.at(self.i)
        self.ref[own] = (
            self.ref[own].astype(F32) + self.wholes[0].astype(F32) + self.wholes[1].astype(F32)
        ).astype(BF)

    def drain(self):
        for r in self.first + self.second:
            r.wait_send()


HA, HB = 80, 80


def mega_kernel(w, hid, q, cot, k, docs, attn, gq, gk, gh, gw,
                wh, hid2, hidt, q2, cot2, kw, vw, dwin, vacc, bias, eb, ds, dob, qs, inv, dl, acc,
                dvb, rv, dkb, rk, o2, dq2, gkb, gvs, ghp, ghr, gho, dw, ha1, wa1, hb1, wb1, ha2, wa2, hb2, wb2,
                yr, zs, zr, fin, pr, wss, wrs, pss, prs, lsem, kss, krs, gss, grs, rss, rrs, yss, yrs):
    me = Where()
    c = me.c
    qcol = lambda n: pl.ds(mo(n * 1280, 128), 1280)
    kcol = lambda n: pl.ds(mo(n * 256, 128), 256)
    hcol = lambda n, g: pl.ds(mo(n * 256 + g * HS, 128), HS)
    local = [
        (k.at[:, hcol(me.core, 0)], kw.at[0, 4, me.core]),
        (docs, dwin.at[4, me.core]),
        (k.at[:, hcol(me.core, 1)], kw.at[1, 4, me.core]),
        (w.at[:, kcol(me.core)], wh.at[me.zl, me.x]),
        (hid, hid2.at[me.core]),
        (q.at[:, qcol(me.core)], q2.at[me.core]),
        (cot.at[:, qcol(me.core)], cot2.at[me.core]),
    ]
    local = [pltpu.make_async_copy(s, d, lsem.at[n]) for n, (s, d) in enumerate(local)]
    for r in local:
        r.start()
    me.enter()
    swap = [
        (k.at[:, hcol(me.other, 0)], kw.at[0, 4, me.core], kw.at[0, 4, me.other]),
        (docs, dwin.at[4, me.core], dwin.at[4, me.other]),
        (k.at[:, hcol(me.other, 1)], kw.at[1, 4, me.core], kw.at[1, 4, me.other]),
        (q.at[:, qcol(me.other)], q2.at[me.core], q2.at[me.other]),
        (cot.at[:, qcol(me.other)], cot2.at[me.core], cot2.at[me.other]),
        (hid, hid2.at[me.core], hid2.at[me.other]),
    ]
    swap_in = [rcopy(s, i, pss.at[n], prs.at[n], me.partner) for n, (s, d, i) in enumerate(swap)]
    swap = [rcopy(s, d, pss.at[n], prs.at[n], me.partner) for n, (s, d, i) in enumerate(swap)]
    for r in swap:
        r.start()

    def swap_out(n, src, dst, into):
        r = rcopy(src, dst, pss.at[n], prs.at[n], me.partner)
        swap.append(r)
        r.start()
        return rcopy(src, into, pss.at[n], prs.at[n], me.partner)

    ra, rb = pl.ds(0, 2 * HA), pl.ds(2 * HA, 2 * HB)
    a0, a1, b0, b1 = pl.ds(0, HA), pl.ds(HA, HA), pl.ds(2 * HA, HB), pl.ds(2 * HA + HB, HB)
    ga1 = Gather4(*[lambda j, r=r: wh.at[me.zl, j, r] for r in (ra, a0, a1)], me.x, me.xp, me.xm, wss.at[0], wrs.at[0])
    gb1 = Gather4(*[lambda j, r=r: wh.at[j, me.x, r] for r in (rb, b0, b1)], me.zl, me.zp, me.zm, wss.at[1], wrs.at[1])
    near = lambda i, n: lax.rem(i + n, 4)
    ga2 = [Gather4(*[lambda j, r=r, n=n: wh.at[j, near(me.x, n), r] for r in (ra, a0, a1)], me.zl, me.zp, me.zm, wss.at[2 + n], wrs.at[2 + n]) for n in range(4)]
    gb2 = [Gather4(*[lambda j, r=r, n=n: wh.at[near(me.zl, n), j, r] for r in (rb, b0, b1)], me.x, me.xp, me.xm, wss.at[6 + n], wrs.at[6 + n]) for n in range(4)]
    sa1 = [Scatter4(dw, *[lambda j, r=r, n=n: (j, near(me.x, n), r) for r in (ra, a0, a1)], me.zl, me.zp, me.zm,
                    ha1.at[n], wa1.at[n], wss.at[10 + n], wrs.at[10 + n]) for n in range(4)]
    sb1 = [Scatter4(dw, *[lambda j, r=r, n=n: (near(me.zl, n), j, r) for r in (rb, b0, b1)], me.x, me.xp, me.xm,
                    hb1.at[n], wb1.at[n], wss.at[14 + n], wrs.at[14 + n]) for n in range(4)]
    sa2 = Scatter4(dw, *[lambda j, r=r: (me.zl, j, r) for r in (ra, a0, a1)], me.x, me.xp, me.xm,
                   ha2, wa2, wss.at[18], wrs.at[18])
    sb2 = Scatter4(dw, *[lambda j, r=r: (j, me.x, r) for r in (rb, b0, b1)], me.zl, me.zp, me.zm,
                   hb2, wb2, wss.at[19], wrs.at[19])

    def spread(buf, n):
        return [(d, rcopy(buf.at[4], buf.at[4 - d], kss.at[n, m], krs.at[n, 4 - d], me.chip(lax.rem(c + d, 8)))) for m, d in enumerate((1, 2, 4))]

    def start_spread(sends):
        for d, r in sends:
            @pl.when(c + d < 8)
            def _():
                r.start()

    passes = (c >= 1) & (c <= 5)

    def forwarding(buf, n):
        return rcopy(buf.at[3], buf.at[1], kss.at[n, 3], krs.at[n, 1], me.chip(lax.rem(c + 2, 8)))

    def arrive(buf, n, j):
        @pl.when(c >= 4 - j)
        def _():
            rcopy(buf.at[4], buf.at[j], kss.at[n, 0], krs.at[n, j], me.chip(lax.rem(c + 4 + j, 8))).wait_recv()

    def forward(buf, n):
        arrive(buf, n, 3)
        @pl.when(passes)
        def _():
            forwarding(buf, n).start()

    def end_spread(buf, n):
        for j in (2, 0, 1):
            arrive(buf, n, j)

    def collecting(buf, into, n, ss, rs):
        to = {0: 4, 1: 2, 2: 2, 3: 1}
        return [rcopy(buf.at[n, j], into.at[n, j], ss.at[n, j], rs.at[n, j], me.chip(lax.rem(c + 8 - to[j], 8))) for j in range(4)]

    def collect(buf, into, n, ss, rs):
        sends = collecting(buf, into, n, ss, rs)
        for j in (1, 0, 2):
            @pl.when(c >= 4 - j)
            def _():
                sends[j].start()
        return sends

    def collect_relay(buf, into, n, ss, rs):
        r = collecting(buf, into, n, ss, rs)
        @pl.when(passes)
        def _():
            r[1].wait_recv()
            buf[n, 3] = (buf[n, 3].astype(F32) + into[n, 1].astype(F32)).astype(BF)
        @pl.when(c >= 1)
        def _():
            r[3].start()

    def collected(buf, into, n, ss, rs):
        acc[...] = buf[n, 4].astype(F32)
        r = collecting(buf, into, n, ss, rs)
        for j, d in ((2, 2), (0, 4), (3, 1)):
            @pl.when(c + d < 8)
            def _():
                r[j].wait_recv()
                acc[...] += into[n, j].astype(F32)
        return acc[...].astype(BF)

    for j in range(4):
        @pl.when(c < 4 - j)
        def _():
            for g in range(2):
                kw[g, j] = jnp.zeros(kw.shape[2:], BF)
                vw[g, j] = jnp.zeros(vw.shape[2:], BF)
            dwin[j] = jnp.full(dwin.shape[1:], -1, jnp.int32)

    flows = [(kw.at[0], 0), (dwin, 1), (kw.at[1], 2), (vw.at[0], 3), (vw.at[1], 4)]
    going = [spread(*f) for f in flows]
    for n in range(3):
        local[n].wait()
        swap_in[n].wait_recv()
        start_spread(going[n])
    local[3].wait()
    ga1.start()
    gb1.start()
    ga2[0].start()
    gb2[0].start()
    for g1, g2 in ((ga1, ga2), (gb1, gb2)):
        g1.relay()
        g2[3].start()
        g2[1].start()
    for g1, g2 in ((ga1, ga2), (gb1, gb2)):
        g1.finish()
        g2[2].start()
    ga2[0].relay()
    gb2[0].relay()
    for f in flows[:3]:
        forward(*f)
    for n in (5, 6):
        local[n].wait()
        swap_in[n - 2].wait_recv()
    end_spread(*flows[0])
    end_spread(*flows[1])
    for n in (3, 1):
        ga2[n].relay()
        gb2[n].relay()
    for t in range(2):
        mine = jnp.transpose(jnp.broadcast_to(dwin[4, t].astype(F32), (BLK, BLK)))
        causal = lax.broadcasted_iota(jnp.int32, (BLK, BLK), 1) <= lax.broadcasted_iota(jnp.int32, (BLK, BLK), 0)
        for b in range(9):
            row = dwin[(b + t) // 2, (b + t) % 2].astype(F32)
            allow = mine == row
            if b == 8:
                allow = allow & causal
            bias[t, :, b * BLK:(b + 1) * BLK] = jnp.where(allow, 0.0, -1e30)

    def window(ref, g, t):
        return ref[g].reshape(1280, HS)[t * BLK:t * BLK + WIN]

    def first(g, t):
        kk = window(kw, g, t)
        for h in range(G):
            n = (g * 2 + t) * G + h
            col = slice((g * G + h) * HS, (g * G + h + 1) * HS)
            hr = slice(h * BLK, (h + 1) * BLK)
            qq = q2[t, :, col]
            s = dott(qq, kk, 1, 1) + bias[t]
            m = jnp.max(s, axis=1, keepdims=True)
            e = jnp.exp2((s - m) * CC)
            iv = 1.0 / jnp.sum(e, axis=1, keepdims=True)
            eb[g * 2 + t, hr, :] = e.astype(BF)
            inv[n] = iv
            dob[g * 2 + t, hr, :] = (cot2[t, :, col].astype(F32) * iv).astype(BF)
            qs[g * 2 + t, hr, :] = qq
        return dott(eb[g * 2 + t], dob[g * 2 + t], 0, 0)

    def put(buf, g, t, part, scale):
        rows = slice(t * BLK, t * BLK + WIN)
        if t == 0:
            dl[rows, :] = part
            dl[WIN:, :] = jnp.zeros((1280 - WIN, HS), F32)
        else:
            dl[rows, :] += part
            buf[g] = (dl[...] * scale).astype(BF).reshape(5, 256, HS)

    def second(g, t):
        kk, vv = window(kw, g, t), window(vw, g, t)
        for h in range(G):
            n = (g * 2 + t) * G + h
            col = slice((g * G + h) * HS, (g * G + h + 1) * HS)
            hr = slice(h * BLK, (h + 1) * BLK)
            iv = inv[n]
            e = eb[g * 2 + t, hr, :]
            ob = (dott(e, vv, 1, 0) * iv).astype(BF)
            o2[t, :, col] = ob
            delta = jnp.sum(cot2[t, :, col].astype(F32) * ob.astype(F32), axis=1, keepdims=True) * iv
            dp = dott(dob[g * 2 + t, hr, :], vv, 1, 1)
            d = (e.astype(F32) * (dp - delta)).astype(BF)
            ds[hr, :] = d
            dq2[t, :, col] = (dott(d, kk, 1, 0) * SCALE).astype(BF)
        return dott(ds[...], qs[g * 2 + t], 0, 0)

    put(dvb, 0, 0, first(0, 0), 1.0)
    put(dvb, 0, 1, first(0, 1), 1.0)
    sends = collect(dvb, rv, 0, gss, grs)
    ga2[2].relay()
    gb2[2].relay()
    end_spread(*flows[2])
    put(dvb, 1, 0, first(1, 0), 1.0)
    put(dvb, 1, 1, first(1, 1), 1.0)
    sends += collect(dvb, rv, 1, gss, grs)
    collect_relay(dvb, rv, 0, gss, grs)
    collect_relay(dvb, rv, 1, gss, grs)
    local[4].wait()
    swap_in[5].wait_recv()
    for n in range(4):
        ga2[n].finish()
        gb2[n].finish()
    for z in range(4):
        h = hid2[:, :, z * 1280:(z + 1) * 1280].reshape(256, 1280)
        part = jnp.dot(h, wh[z].reshape(1280, 256), preferred_element_type=F32)
        vacc[...] = part if z == 0 else vacc[...] + part
    for g in range(2):
        vw[g, 4] = vacc[:, g * HS:(g + 1) * HS].astype(BF).reshape(2, 128, HS)
    start_spread(going[3])
    start_spread(going[4])
    for z in range(4):
        hidt[z * 1280:(z + 1) * 1280, :] = jnp.transpose(hid2[:, :, z * 1280:(z + 1) * 1280].reshape(256, 1280))
    for g in range(2):
        gvs[:, :, g * HS:(g + 1) * HS] = collected(dvb, rv, g, gss, grs).reshape(2, 128, HS)
    gv = gvs[...].reshape(256, 256)
    order = (2, 1, 3, 0)
    for n in order:
        z = near(me.zl, n)
        dw[z] = jnp.dot(hidt[pl.ds(mo(z * 1280, 128), 1280), :], gv, preferred_element_type=F32).astype(BF).reshape(4, 320, 256)
        sb1[n].start()
    for n in order:
        sa1[n].start()
    forward(*flows[3])
    forward(*flows[4])
    for z in range(4):
        ghp[:, z * 1280:(z + 1) * 1280] = dott(gvs[me.other], wh[z].reshape(1280, 256), 1, 1).astype(BF)
    gh_in = swap_out(6, ghp, ghr, ghr)
    for n in order:
        sa1[n].relay()
        sb1[n].relay()
    end_spread(*flows[3])
    put(dkb, 0, 0, second(0, 0), SCALE)
    sa1[2].finish()
    sa2.start()
    sb1[2].finish()
    sb2.start()
    put(dkb, 0, 1, second(0, 1), SCALE)
    sends += collect(dkb, rk, 0, rss, rrs)
    for n in (1, 3):
        sa1[n].finish()
        sb1[n].finish()
    sa2.relay()
    sb2.relay()
    end_spread(*flows[4])
    put(dkb, 1, 0, second(1, 0), SCALE)
    sa1[0].finish()
    sb1[0].finish()
    sa2.finish()
    sb2.finish()
    piece = lambda j: dw.at[me.zl, me.x, pl.ds(mo(j * 80, 16), 80)]
    ychip = lambda d: me.chip(lax.rem(me.y + d, 4) * 2 + me.zh)
    ysend = [rcopy(piece(lax.rem(me.y + d, 4)), yr.at[d - 1], yss.at[d - 1], yrs.at[d - 1], ychip(d)) for d in range(1, 4)]
    for r in ysend:
        r.start()
    collect_relay(dkb, rk, 0, rss, rrs)
    put(dkb, 1, 1, second(1, 1), SCALE)
    sends += collect(dkb, rk, 1, rss, rrs)
    tot = dw[me.zl, me.x, pl.ds(mo(me.y * 80, 16), 80)].astype(F32)
    for d in range(3):
        ysend[d].wait_recv()
        tot = tot + yr[d].astype(F32)
    zs[...] = tot.astype(BF)
    zx = rcopy(zs, zr, yss.at[3], yrs.at[3], me.chip(me.y * 2 + 1 - me.zh))
    zx.start()
    o_in = swap_out(7, o2.at[me.other], attn.at[:, qcol(me.core)], attn.at[:, qcol(me.other)])
    dq_in = swap_out(8, dq2.at[me.other], gq.at[:, qcol(me.core)], gq.at[:, qcol(me.other)])
    tail = [(o2.at[me.core], attn.at[:, qcol(me.core)]), (dq2.at[me.core], gq.at[:, qcol(me.core)])]
    tail = [pltpu.make_async_copy(s, d, lsem.at[n]) for n, (s, d) in enumerate(tail)]
    for r in tail:
        r.start()
    for z in range(4):
        cols = slice(z * 1280, (z + 1) * 1280)
        gho[:, cols] = dott(gvs[me.core], wh[z].reshape(1280, 256), 1, 1)
    collect_relay(dkb, rk, 1, rss, rrs)
    gh_in.wait_recv()
    gh[...] = (gho[...] + ghr[...].astype(F32)).astype(BF)
    zx.wait_recv()
    fin[me.y] = (zs[...].astype(F32) + zr[...].astype(F32)).astype(BF)
    ysend2 = [rcopy(fin.at[me.y], fin.at[me.y], yss.at[3 + d], yrs.at[3 + d], ychip(d)) for d in range(1, 4)]
    for r in ysend2:
        r.start()
    w_in = [swap_out(10, fin.at[me.y], pr.at[me.y], pr.at[me.y])]
    for g in range(2):
        gkb[:, :, g * HS:(g + 1) * HS] = collected(dkb, rk, g, rss, rrs).reshape(2, 128, HS)
    gk_in = swap_out(9, gkb.at[me.other], gk.at[:, kcol(me.core)], gk.at[:, kcol(me.other)])
    last = pltpu.make_async_copy(gkb.at[me.core], gk.at[:, kcol(me.core)], lsem.at[2])
    last.start()
    for d in range(1, 4):
        j = lax.rem(me.y + 4 - d, 4)
        rcopy(fin.at[j], fin.at[j], yss.at[3 + d], yrs.at[3 + d], ychip(d)).wait_recv()
        w_in.append(swap_out(10 + d, fin.at[j], pr.at[j], pr.at[j]))
    gw[:, kcol(me.core)] = fin[...].astype(F32).reshape(320, 256)
    for r in w_in:
        r.wait_recv()
    gw[:, kcol(me.other)] = pr[...].astype(F32).reshape(320, 256)
    for r in tail + [last]:
        r.wait()
    for r in (o_in, dq_in, gk_in):
        r.wait_recv()
    for r in swap + ysend + ysend2 + [zx]:
        r.wait_send()
    for f, p in zip(flows, going):
        for d, r in p:
            @pl.when(c + d < 8)
            def _():
                r.wait_send()
        @pl.when(passes)
        def _():
            forwarding(*f).wait_send()
    for n, r in enumerate(sends):
        @pl.when(c >= 4 - n % 4)
        def _():
            r.wait_send()
    for g in (ga1, gb1, *ga2, *gb2, *sa1, *sb1, sa2, sb2):
        g.drain()


def mega(w, hid, q, cot, k, docs):
    shp = jax.ShapeDtypeStruct
    vm = pl.BlockSpec(memory_space=pltpu.VMEM)
    dma = pltpu.SemaphoreType.DMA
    v = pltpu.VMEM
    return pl.pallas_call(
        mega_kernel,
        out_shape=(
            shp((128, 2560), BF), shp((128, 2560), BF), shp((128, 512), BF), shp((128, 5120), BF), shp((320, 512), F32),
        ),
        in_specs=[pl.BlockSpec(memory_space=pltpu.HBM)] * 6,
        out_specs=(vm,) * 5,
        scratch_shapes=[
            v((4, 4, 320, 256), BF), v((2, 128, 5120), BF), v((5120, 256), BF), v((2, 128, 1280), BF), v((2, 128, 1280), BF),
            v((2, 5, 2, 128, HS), BF), v((2, 5, 2, 128, HS), BF), v((5, 2, 1, 128), jnp.int32), v((256, 256), F32),
            v((2, BLK, WIN), F32), v((4, G * BLK, WIN), BF), v((G * BLK, WIN), BF), v((4, G * BLK, HS), BF), v((4, G * BLK, HS), BF),
            v((20, BLK, 1), F32), v((1280, HS), F32), v((256, HS), F32),
            v((2, 5, 256, HS), BF), v((2, 4, 256, HS), BF), v((2, 5, 256, HS), BF), v((2, 4, 256, HS), BF),
            v((2, 128, 1280), BF), v((2, 128, 1280), BF), v((2, 128, 256), BF), v((2, 128, 256), BF),
            v((128, 5120), BF), v((128, 5120), BF), v((128, 5120), F32), v((4, 4, 320, 256), BF),
            v((4, 2, HA, 256), BF), v((4, 2, 2 * HA, 256), BF), v((4, 2, HB, 256), BF), v((4, 2, 2 * HB, 256), BF),
            v((2, HA, 256), BF), v((2, 2 * HA, 256), BF), v((2, HB, 256), BF), v((2, 2 * HB, 256), BF),
            v((3, 80, 256), BF), v((80, 256), BF), v((80, 256), BF), v((4, 80, 256), BF), v((4, 80, 256), BF),
            dma((20, 4)), dma((20, 4)), dma((14,)), dma((14,)), dma((7,)), dma((5, 4)), dma((5, 4)),
            dma((2, 4)), dma((2, 4)), dma((2, 4)), dma((2, 4)), dma((7,)), dma((7,)),
        ],
        compiler_params=pltpu.CompilerParams(collective_id=0, has_side_effects=True, vmem_limit_bytes=44 << 20),
        name="whole",
    )(w, hid, q, cot, k, docs)


def flush_kernel(*refs):
    sem = refs[10]
    copies = [pltpu.make_async_copy(refs[n], refs[5 + n], sem.at[n]) for n in range(5)]
    for r in copies:
        r.start()
    for r in copies:
        r.wait()


def flush(*arrays):
    return pl.pallas_call(
        flush_kernel,
        out_shape=tuple(jax.ShapeDtypeStruct(a.shape, a.dtype) for a in arrays),
        in_specs=[pl.BlockSpec(memory_space=pltpu.VMEM)] * 5,
        out_specs=(pl.BlockSpec(memory_space=pl.ANY),) * 5,
        scratch_shapes=[pltpu.SemaphoreType.DMA((5,))],
        compiler_params=pltpu.CompilerParams(vmem_limit_bytes=4 << 20),
        name="flush",
    )(*arrays)


def body(hidden, queries, keys, value_weight, doc_ids, cotangent):
    attn, gq, gk, gh, gw = flush(*mega(*[pltpu.with_memory_space_constraint(a, pltpu.HBM) for a in (value_weight, hidden[0], queries[0], cotangent[0], keys[0], doc_ids)]))
    return attn[None], gq[None], gk[None], gh[None], gw


def solution(mesh):
    rows = P("dp", "seq", None)
    return jax.shard_map(
        body, mesh=mesh,
        in_specs=(rows, rows, rows, P("dp", None), P("dp", "seq"), rows),
        out_specs=(rows, rows, rows, rows, P("dp", None)),
        check_vma=False,
    )
```
